256 devices in a mesh: pix: 32 (over z_hi, y, x), tm: 8 (over z_lo, core).
Axes of the slice: x: 4, y: 4, z: 8 (z_hi: 2, z_lo: 4; z = z_hi * 4 + z_lo), core: 2. Of those that a mesh axis runs over, the one named last changes fastest.
Arguments:
- fields: float32 [256, 8, 2, 1024], P('pix', None, None, 'tm'), may hold values from -6 to 6
- profiles: bfloat16 [65536, 256], P('pix'), may hold values from -0.75 to 0.75
- phase: float32 [256, 1024], P(('pix', 'tm')), may hold values from -3.140625 to 3.140625
Outputs:
- advanced: float32 [256, 8, 2, 1024], P('pix', None, None, 'tm')
The draws below stay inside these ranges and needn't reach their ends.
All inputs are finite; a program needn't handle non-finite values.
Results may differ from the reference program's by a relative error of at most 0.003.
Values may be sent and summed in bfloat16 or wider, within the bound.
A program may use at most 64 MiB of HBM per device.

```python
import math
import jax
import jax.numpy as jnp
from jax import lax

MODES = 256
TIMES = 1024
PIX_DEV = 2048
BATCH = 8
PIXELS = 65536


def raised(array, own_key, source, target, parts, factor):
    owner, partner = [(jnp.arange(array.shape[position]) // (array.shape[position] // parts)).reshape([-1 if axis == position else 1 for axis in range(array.ndim)]) for position in (source, target)]
    chosen = jax.random.permutation(own_key, parts)[partner]
    strong = (owner == chosen) | (owner == (partner + parts // 2) % parts)
    return jnp.where(strong, factor * array, array)


def steps_of(own_key, shape, cuts, least, largest):
    factor_of = 1.0
    for axis_at, parts in cuts:
        steps = jax.random.uniform(jax.random.fold_in(jax.random.fold_in(own_key, 6), axis_at), (parts,), jnp.float32, least / len(cuts), largest / len(cuts))
        factor_of = factor_of * jnp.repeat(jnp.exp(steps), shape[axis_at] // parts).reshape((-1,) + (1,) * (len(shape) - 1 - axis_at))
    return factor_of


def normal_values(rng, dims, spread, most, cuts=(), held_as=jnp.bfloat16):
    loudness = steps_of(rng, dims, cuts, -0.22, 0.18) if cuts else 1.0
    array = jax.random.normal(rng, dims, jnp.float32) * spread * loudness
    return jnp.minimum(jnp.maximum(array, -most), most).astype(held_as)


def noise_with(own_key, extent, deviation, bound, split, heavy, kind=jnp.bfloat16):
    entries = deviation * jax.random.normal(own_key, extent, jnp.float32)
    if split:
        entries = entries * steps_of(own_key, extent, split, -0.22, 0.18)
    return jnp.clip(raised(entries, jax.random.fold_in(own_key, 3), *heavy), -bound, bound).astype(kind)


def setup_inputs(seed: int = 0) -> dict:
    streams_of = jax.random.split(jax.random.key(seed), 4)
    return {
        "fields": normal_values(streams_of[0], (MODES, BATCH, 2, TIMES), 1.0, 6.0, ((0, 32), (3, 8)), jnp.float32),
        "profiles": noise_with(streams_of[1], (PIXELS, MODES), MODES ** -0.5, 0.75, ((0, 32),), (0, 1, 32, 2.75)),
        "phase": jnp.clip(jax.random.uniform(streams_of[2], (MODES, TIMES), jnp.float32, -3.140625, 3.140625), -3.140625, 3.140625),
    }


def reference(fields, profiles, phase):
    count = profiles.shape[0]
    modes = fields.shape[0]
    block = PIX_DEV
    flat = fields.astype(jnp.bfloat16).reshape(modes, -1)

    def visit(total, start):
        rows = lax.dynamic_slice_in_dim(profiles, start, block, 0)
        spatial = jnp.dot(rows, flat, preferred_element_type=jnp.float32).reshape(block, BATCH, 2, TIMES)
        real_part = spatial[:, :, 0]
        imag_part = spatial[:, :, 1]
        power = real_part * real_part + imag_part * imag_part
        nonlin = jnp.stack([power * real_part, power * imag_part], axis=2).astype(jnp.bfloat16).reshape(block, -1)
        total = total + lax.dot_general(rows, nonlin, (((0,), (0,)), ((), ())), preferred_element_type=jnp.float32)
        return (total, None)
    starts = jnp.arange(count // block, dtype=jnp.int32) * block
    kerr, unused = lax.scan(visit, jnp.zeros((modes, BATCH * 2 * TIMES), jnp.float32), starts)
    kerr = kerr.reshape(modes, BATCH, 2, TIMES) * (1.0 / math.sqrt(count))
    stepped_re = fields[:, :, 0] - kerr[:, :, 1]
    stepped_im = fields[:, :, 1] + kerr[:, :, 0]
    spectrum = jnp.fft.fft(stepped_re + 1j * stepped_im, axis=-1)
    rotated = spectrum * jnp.exp(1j * phase)[:, None, :]
    result = jnp.fft.ifft(rotated, axis=-1)
    return jnp.stack([jnp.real(result), jnp.imag(result)], axis=2).astype(jnp.float32)
```

```python
import functools
import math

import jax
import jax.numpy as jnp
import numpy as np
from jax import lax
from jax.experimental import pallas as pl
from jax.experimental.pallas import tpu as pltpu
from jax.sharding import PartitionSpec as P

MESH = pl.DeviceIdType.MESH
F32 = jnp.float32
BF16 = jnp.bfloat16

SLOTS = ((2, 0), (2, 1), (1, 0), (1, 1), (3, 0), (3, 1), (0, 1), (0, 0))
TILE = 512


def tables():
    row = np.arange(256)
    order = (row // 8 % 2) * 128 + (row // 16) * 8 + row % 8
    perm = np.zeros((256, 256), np.float32)
    perm[order, row] = 1.0
    angle = 2.0 * np.pi * (np.outer(np.arange(128), np.arange(128)) % 128) / 128.0
    cos, sin = np.cos(angle), np.sin(angle)
    dft = np.block([[cos, -sin], [sin, cos]]).astype(np.float32)
    high = dft.astype(jnp.bfloat16)
    low = (dft - high.astype(np.float32)).astype(jnp.bfloat16)
    turn = 2.0 * np.pi * np.outer(np.arange(8), np.arange(128)) / 1024.0
    twist = np.concatenate([np.cos(turn), np.sin(turn)]).astype(np.float32)
    square = np.stack([perm.astype(jnp.bfloat16), high, low])
    return square, twist


def fft8(re, im, sign):
    half = math.sqrt(0.5)

    def turned(x, y, k):
        if k == 0:
            return x, y
        if k == 1:
            return (x - sign * y) * half, (y + sign * x) * half
        if k == 2:
            return (-y, x) if sign > 0 else (y, -x)
        return (-x - sign * y) * half, (-y + sign * x) * half

    def four(r, i):
        ar, ai, br, bi = r[0] + r[2], i[0] + i[2], r[0] - r[2], i[0] - i[2]
        cr, ci, dr, di = r[1] + r[3], i[1] + i[3], r[1] - r[3], i[1] - i[3]
        dr, di = turned(dr, di, 2)
        return [ar + cr, br + dr, ar - cr, br - dr], [ai + ci, bi + di, ai - ci, bi - di]

    er, ei = four(re[0::2], im[0::2])
    od, oi = four(re[1::2], im[1::2])
    out_re, out_im = [None] * 8, [None] * 8
    for k in range(4):
        tr, ti = turned(od[k], oi[k], k)
        out_re[k], out_im[k] = er[k] + tr, ei[k] + ti
        out_re[k + 4], out_im[k + 4] = er[k] - tr, ei[k] - ti
    return out_re, out_im


def split(value):
    high = value.astype(BF16)
    return high, (value - high.astype(F32)).astype(BF16)


def dot(a, b, dims=((1,), (0,))):
    return lax.dot_general(a, b, (dims, ((), ())), preferred_element_type=F32)


def kernel(
    f_hbm, p_hbm, ph_hbm, sq_hbm, tw_hbm, o_ref,
    f_v, p_v, ph_v, sq_v, tw_v, pm_v, pt_v, mbuf, s_hi, s_lo, a1, lo, cs_s, cs_r,
    kf, ks, kr1, kown, k1s, kr2, kmid, kx, esf, esb, erf, erb,
    in_sem, a1s, a1r, los, lor, css, csr, a2s, a2r, c1s, c1r, efs, efr, ebs, ebr,
):
    pix, tm = lax.axis_index("pix"), lax.axis_index("tm")
    zh, y, x = pix // 16, (pix // 4) % 4, pix % 4
    yx = pix % 16
    zl, core = tm // 2, tm % 2
    other = 1 - zh
    here = zh * 8 + tm

    def at_z(h, t):
        return (h * 16 + yx, t)

    def at_x(k):
        return (zh * 16 + y * 4 + lax.rem(x + k, 4), tm)

    def at_y(k):
        return (zh * 16 + lax.rem(y + k, 4) * 4 + x, tm)

    def remote(src, dst, ss, rs, device):
        return pltpu.make_async_remote_copy(
            src_ref=src, dst_ref=dst, send_sem=ss, recv_sem=rs, device_id=device, device_id_type=MESH
        )

    def column(o):
        peer = lax.rem(here + o, 16)
        return peer // 8, lax.rem(peer, 8)

    sends = []

    def send(*a):
        copy = remote(*a)
        copy.start()
        sends.append(copy)

    def arrive(ref, rs):
        remote(ref, ref, rs, rs, at_x(1)).wait_recv()

    barrier = pltpu.get_barrier_semaphore()
    for o in range(1, 16):
        h, t = column(o)
        pl.semaphore_signal(barrier, inc=1, device_id=at_z(h, t), device_id_type=MESH)
    for k in range(1, 4):
        pl.semaphore_signal(barrier, inc=1, device_id=at_x(k), device_id_type=MESH)
        pl.semaphore_signal(barrier, inc=1, device_id=at_y(k), device_id_type=MESH)

    loads = [
        pltpu.make_async_copy(src, dst, in_sem.at[n])
        for n, (src, dst) in enumerate(
            ((f_hbm, f_v), (ph_hbm, ph_v), (sq_hbm, sq_v), (p_hbm, p_v), (tw_hbm, tw_v))
        )
    ]
    for load in loads:
        load.start()

    loads[0].wait()
    for b in range(8):
        value = jnp.concatenate([f_v[pl.ds(2 * b + c, 8, stride=16), :] for c in range(2)], axis=0)
        high, low = split(value)
        s_hi[b] = high
        s_lo[b] = low
    a1[here] = s_hi[tm]
    lo[tm] = s_lo[tm]

    pl.semaphore_wait(barrier, 21)
    for o in (8, 7, 9, 6, 10, 5, 11, 4, 12, 3, 13, 2, 14, 1, 15):
        h, t = column(o)
        send(s_hi.at[t], a1.at[here], a1s.at[o], a1r.at[here], at_z(h, t))

    loads[1].wait()
    lane = lax.broadcasted_iota(jnp.int32, (8, 128), 1)
    sub = lax.broadcasted_iota(jnp.int32, (8, 128), 0)
    chosen = lax.rem(lane, 8) == sub
    rows = []
    for k in range(8):
        spread = jnp.where(chosen, jnp.broadcast_to(ph_v[k : k + 1, :], (8, 128)), 0.0)
        first, rest = split(spread)
        second = rest.astype(F32)
        third = spread - first.astype(F32) - second
        rows += [first.astype(F32), second, third]
    gather_lane = lax.broadcasted_iota(jnp.int32, (128, 128), 0) // 8
    gather = (gather_lane == lax.broadcasted_iota(jnp.int32, (128, 128), 1)).astype(F32).astype(BF16)
    packed = dot(jnp.concatenate(rows, axis=0).astype(BF16), gather)
    angle = jnp.zeros((8, 128), F32)
    for k in range(8):
        part = packed[24 * k : 24 * k + 8] + packed[24 * k + 8 : 24 * k + 16] + packed[24 * k + 16 : 24 * k + 24]
        angle = angle + (part if k == 0 else pltpu.roll(part, 16 * k, 1))
    cs_s[0:8, :] = jnp.cos(angle)
    cs_s[8:16, :] = jnp.sin(angle)
    mine = pl.ds(pl.multiple_of(here * 16, 16), 16)
    cs_r[mine, :] = cs_s[...]
    for o in range(1, 8):
        t = lax.rem(tm + o, 8)
        send(s_lo.at[t], lo.at[tm], los.at[o], lor.at[tm], at_z(zh, t))
    for o in range(1, 16):
        h, t = column(o)
        send(cs_s, cs_r.at[mine], css.at[o], csr.at[here], at_z(h, t))

    loads[2].wait()
    loads[3].wait()
    for n in range(2048 // TILE):
        block = p_v[n * TILE : (n + 1) * TILE, :]
        pm_v[n] = dot(block, sq_v[0]).astype(BF16)
        pt_v[n] = dot(sq_v[0], block, ((0,), (1,))).astype(BF16)

    blocks = [lax.rem(zl + step, 4) * 2 + lax.rem(core + c, 2) for step, c in SLOTS]

    for n, a in enumerate(blocks):
        if SLOTS[n] != (0, 0):
            arrive(a1.at[zh * 8 + a], a1r.at[zh * 8 + a])
        arrive(a1.at[other * 8 + a], a1r.at[other * 8 + a])
        first, second = a1[a].astype(F32), a1[8 + a].astype(F32)
        for c in range(2):
            both = jnp.concatenate([first[8 * c : 8 * c + 8], second[8 * c : 8 * c + 8]], axis=0)
            mbuf[a, c, y, x] = both.astype(BF16)
        piece = mbuf.at[a, :, y, x]
        for k in range(1, 4):
            send(piece, piece, a2s.at[n, k - 1], a2r.at[n, k - 1], at_x(k) if n % 2 == 0 else at_y(k))

    def second_leg(n):
        a = blocks[n]
        for k in range(1, 4):
            at = (y, lax.rem(x + 4 - k, 4)) if n % 2 == 0 else (lax.rem(y + 4 - k, 4), x)
            arrive(mbuf.at[a, :, at[0], at[1]], a2r.at[n, k - 1])
        piece = mbuf.at[a, :, y] if n % 2 == 0 else mbuf.at[a, :, :, x]
        for k in range(1, 4):
            send(piece, piece, a2s.at[n, k + 2], a2r.at[n, k + 2], at_y(k) if n % 2 == 0 else at_x(k))

    def compute(n):
        a = blocks[n]
        for k in range(1, 4):
            if n % 2 == 0:
                piece = mbuf.at[a, :, lax.rem(y + 4 - k, 4)]
            else:
                piece = mbuf.at[a, :, :, lax.rem(x + 4 - k, 4)]
            arrive(piece, a2r.at[n, k + 2])
        fields = jnp.concatenate([mbuf[a, c].reshape(256, 128) for c in range(2)], axis=1)
        total = None
        for t in range(2048 // TILE):
            spatial = dot(pm_v[t], fields)
            re, im = spatial[:, :128], spatial[:, 128:]
            power = re * re + im * im
            nonlin = jnp.concatenate([power * re, power * im], axis=1).astype(BF16)
            part = dot(pt_v[t], nonlin)
            total = part if total is None else total + part
        for c in range(2):
            half = total[:, 128 * c : 128 * c + 128].reshape(4, 4, 16, 128)
            kf[n, c] = half
            ks[n, c] = half.astype(BF16)
        for k in range(1, 4):
            if n % 2 == 0:
                piece, to = ks.at[n, :, :, lax.rem(x + k, 4)], at_x(k)
            else:
                piece, to = ks.at[n, :, lax.rem(y + k, 4)], at_y(k)
            send(piece, kr1.at[n, k - 1], c1s.at[n, k - 1], c1r.at[n, k - 1], to)

    def reduce_first(n):
        for k in range(3):
            arrive(kr1.at[n, k], c1r.at[n, k])
        total = kf[n, :, :, x] if n % 2 == 0 else kf[n, :, y]
        for k in range(3):
            total = total + kr1[n, k].astype(F32)
        kmid[n] = total
        k1s[n] = total.astype(BF16)
        for k in range(1, 4):
            if n % 2 == 0:
                piece, to = k1s.at[n, :, lax.rem(y + k, 4)], at_y(k)
            else:
                piece, to = k1s.at[n, :, lax.rem(x + k, 4)], at_x(k)
            send(piece, kr2.at[n, k - 1], c1s.at[n, k + 2], c1r.at[n, k + 2], to)

    def reduce_second(n):
        for k in range(3):
            arrive(kr2.at[n, k], c1r.at[n, k + 3])
        total = kmid[n, :, y] if n % 2 == 0 else kmid[n, :, x]
        for k in range(3):
            total = total + kr2[n, k].astype(F32)
        kx[blocks[n]] = total

    second_leg(0)
    second_leg(1)
    for n in range(8):
        if n + 2 < 8:
            second_leg(n + 2)
        compute(n)
        if n >= 3:
            reduce_first(n - 3)
        if n >= 6:
            reduce_second(n - 6)
    for n in range(5, 8):
        reduce_first(n)
        reduce_second(n - 3)
    for n in range(5, 8):
        reduce_second(n)

    loads[4].wait()
    for o in range(1, 8):
        t = lax.rem(tm + o, 8)
        arrive(lo.at[t], lor.at[t])
    for o in range(1, 16):
        h, t = column(o)
        peer = h * 8 + t
        arrive(cs_r.at[pl.ds(pl.multiple_of(peer * 16, 16), 16)], csr.at[peer])
    scale = 1.0 / math.sqrt(65536.0)
    at_low = jnp.where(zh == 0, 1.0, 0.0).astype(F32)
    at_high = 1.0 - at_low
    step_re, step_im = [], []
    for a in range(8):
        own = a1[zh * 8 + a].astype(F32) + lo[a].astype(F32)
        own_re = jnp.concatenate([own[:8] * at_low, own[:8] * at_high], axis=0)
        own_im = jnp.concatenate([own[8:] * at_low, own[8:] * at_high], axis=0)
        step_re.append(own_re - kx[a, 1] * scale)
        step_im.append(own_im + kx[a, 0] * scale)
    fre, fim = fft8(step_re, step_im, -1)
    turned = []
    for r in range(8):
        cos, sin = tw_v[r : r + 1, :], tw_v[8 + r : 9 + r, :]
        turned.append(jnp.concatenate([fre[r] * cos + fim[r] * sin, fim[r] * cos - fre[r] * sin], axis=1))
    high, low = split(jnp.concatenate(turned, axis=0))
    freq = dot(high, sq_v[1]) + dot(low, sq_v[1]) + dot(high, sq_v[2])
    spun = []
    for r in range(8):
        cos, sin = cs_r[pl.ds(r, 16, stride=16), :], cs_r[pl.ds(8 + r, 16, stride=16), :]
        re, im = freq[16 * r : 16 * r + 16, :128], freq[16 * r : 16 * r + 16, 128:]
        spun.append(jnp.concatenate([re * cos - im * sin, re * sin + im * cos], axis=1))
    high, low = split(jnp.concatenate(spun, axis=0))
    back_dims = ((1,), (1,))
    back = dot(high, sq_v[1], back_dims) + dot(low, sq_v[1], back_dims) + dot(high, sq_v[2], back_dims)
    again_re, again_im = [], []
    for r in range(8):
        cos, sin = tw_v[r : r + 1, :] * (1.0 / 1024.0), tw_v[8 + r : 9 + r, :] * (1.0 / 1024.0)
        re, im = back[16 * r : 16 * r + 16, :128], back[16 * r : 16 * r + 16, 128:]
        again_re.append(re * cos - im * sin)
        again_im.append(im * cos + re * sin)
    out_re, out_im = fft8(again_re, again_im, 1)

    for a in range(8):
        low_half = jnp.concatenate([out_re[a][:8], out_im[a][:8]], axis=0)
        high_half = jnp.concatenate([out_re[a][8:], out_im[a][8:]], axis=0)
        esf[a] = low_half * at_low + high_half * at_high
        esb[a] = (low_half * at_high + high_half * at_low).astype(BF16)
    for o in range(8):
        t = lax.rem(tm + o, 8)
        send(esb.at[t], erb.at[tm], ebs.at[o], ebr.at[tm], at_z(other, t))
    for o in range(1, 8):
        t = lax.rem(tm + o, 8)
        send(esf.at[t], erf.at[tm], efs.at[o], efr.at[tm], at_z(zh, t))
    erf[tm] = esf[tm]
    for o in range(8):
        t = lax.rem(tm + o, 8)
        if o:
            arrive(erf.at[t], efr.at[t])
        arrive(erb.at[t], ebr.at[t])
    for b in range(8):
        value = erf[b] + erb[b].astype(F32)
        for c in range(2):
            o_ref[pl.ds(2 * b + c, 8, stride=16), :] = value[8 * c : 8 * c + 8]
    for copy in sends:
        copy.wait_send()


def body(fields, profiles, phase):
    square, twist = tables()
    dma = pltpu.SemaphoreType.DMA
    any_spec = pl.BlockSpec(memory_space=pl.ANY)
    out = pl.pallas_call(
        kernel,
        out_shape=jax.ShapeDtypeStruct((128, 128), F32),
        in_specs=[any_spec] * 5,
        out_specs=pl.BlockSpec(memory_space=pltpu.VMEM),
        scratch_shapes=[
            pltpu.VMEM((128, 128), F32),
            pltpu.VMEM((2048, 256), BF16),
            pltpu.VMEM((8, 128), F32),
            pltpu.VMEM((3, 256, 256), BF16),
            pltpu.VMEM((16, 128), F32),
            pltpu.VMEM((2048 // TILE, TILE, 256), BF16),
            pltpu.VMEM((2048 // TILE, 256, TILE), BF16),
            pltpu.VMEM((8, 2, 4, 4, 16, 128), BF16),
            pltpu.VMEM((8, 16, 128), BF16),
            pltpu.VMEM((8, 16, 128), BF16),
            pltpu.VMEM((16, 16, 128), BF16),
            pltpu.VMEM((8, 16, 128), BF16),
            pltpu.VMEM((16, 128), F32),
            pltpu.VMEM((256, 128), F32),
            pltpu.VMEM((8, 2, 4, 4, 16, 128), F32),
            pltpu.VMEM((8, 2, 4, 4, 16, 128), BF16),
            pltpu.VMEM((8, 3, 2, 4, 16, 128), BF16),
            pltpu.VMEM((8, 128), F32),
            pltpu.VMEM((8, 2, 4, 16, 128), BF16),
            pltpu.VMEM((8, 3, 2, 16, 128), BF16),
            pltpu.VMEM((8, 2, 4, 16, 128), F32),
            pltpu.VMEM((8, 2, 16, 128), F32),
            pltpu.VMEM((8, 16, 128), F32),
            pltpu.VMEM((8, 16, 128), BF16),
            pltpu.VMEM((8, 16, 128), F32),
            pltpu.VMEM((8, 16, 128), BF16),
            dma((5,)),
            dma((16,)), dma((16,)),
            dma((8,)), dma((8,)),
            dma((16,)), dma((16,)),
            dma((8, 6)), dma((8, 6)),
            dma((8, 6)), dma((8, 6)),
            dma((8,)), dma((8,)),
            dma((8,)), dma((8,)),
        ],
        compiler_params=pltpu.CompilerParams(
            collective_id=0, has_side_effects=True, vmem_limit_bytes=40 * 1024 * 1024
        ),
    )(fields.reshape(128, 128), profiles, phase.reshape(8, 128), jnp.asarray(square), jnp.asarray(twist))
    return out.reshape(8, 8, 2, 128)


def solution(mesh):
    return jax.shard_map(
        body,
        mesh=mesh,
        in_specs=(P("pix", None, None, "tm"), P("pix", None), P(("pix", "tm"), None)),
        out_specs=P("pix", None, None, "tm"),
        check_vma=False,
    )
```

```python
import functools
import math

import jax
import jax.numpy as jnp
import numpy as np
from jax import lax
from jax.experimental import pallas as pl
from jax.experimental.pallas import tpu as pltpu
from jax.sharding import PartitionSpec as P

MESH = pl.DeviceIdType.MESH
F32 = jnp.float32
BF16 = jnp.bfloat16

SLOTS = ((2, 0), (2, 1), (1, 0), (1, 1), (3, 0), (3, 1), (0, 1), (0, 0))
TILE = 512


def tables():
    row = np.arange(256)
    order = (row // 8 % 2) * 128 + (row // 16) * 8 + row % 8
    perm = np.zeros((256, 256), np.float32)
    perm[order, row] = 1.0
    angle = 2.0 * np.pi * (np.outer(np.arange(128), np.arange(128)) % 128) / 128.0
    cos, sin = np.cos(angle), np.sin(angle)
    dft = np.block([[cos, -sin], [sin, cos]]).astype(np.float32)
    high = dft.astype(jnp.bfloat16)
    low = (dft - high.astype(np.float32)).astype(jnp.bfloat16)
    turn = 2.0 * np.pi * np.outer(np.arange(8), np.arange(128)) / 1024.0
    twist = np.concatenate([np.cos(turn), np.sin(turn)]).astype(np.float32)
    square = np.stack([perm.astype(jnp.bfloat16), high, low])
    return square, twist


def fft8(re, im, sign):
    half = math.sqrt(0.5)

    def turned(x, y, k):
        if k == 0:
            return x, y
        if k == 1:
            return (x - sign * y) * half, (y + sign * x) * half
        if k == 2:
            return (-y, x) if sign > 0 else (y, -x)
        return (-x - sign * y) * half, (-y + sign * x) * half

    def four(r, i):
        ar, ai, br, bi = r[0] + r[2], i[0] + i[2], r[0] - r[2], i[0] - i[2]
        cr, ci, dr, di = r[1] + r[3], i[1] + i[3], r[1] - r[3], i[1] - i[3]
        dr, di = turned(dr, di, 2)
        return [ar + cr, br + dr, ar - cr, br - dr], [ai + ci, bi + di, ai - ci, bi - di]

    er, ei = four(re[0::2], im[0::2])
    od, oi = four(re[1::2], im[1::2])
    out_re, out_im = [None] * 8, [None] * 8
    for k in range(4):
        tr, ti = turned(od[k], oi[k], k)
        out_re[k], out_im[k] = er[k] + tr, ei[k] + ti
        out_re[k + 4], out_im[k + 4] = er[k] - tr, ei[k] - ti
    return out_re, out_im


def split(value):
    high = value.astype(BF16)
    return high, (value - high.astype(F32)).astype(BF16)


def dot(a, b, dims=((1,), (0,))):
    return lax.dot_general(a, b, (dims, ((), ())), preferred_element_type=F32)


def kernel(
    f_hbm, p_hbm, ph_hbm, sq_hbm, tw_hbm, o_ref,
    f_v, p_v, ph_v, sq_v, tw_v, pm_v, pt_v, mbuf, s_hi, s_lo, a1, lo, cs_s, cs_r,
    kf, ks, kr1, k1s, kr2, kmid, kx, esf, esb, erf, erb,
    in_sem, out_sem, a1r, lor, csr, a2r, c1r, e_sem,
):
    pix, tm = lax.axis_index("pix"), lax.axis_index("tm")
    zh, y, x = pix // 16, (pix // 4) % 4, pix % 4
    yx = pix % 16
    zl, core = tm // 2, tm % 2
    other = 1 - zh
    here = zh * 8 + tm

    def at_z(h, t):
        return (h * 16 + yx, t)

    def at_x(k):
        return (zh * 16 + y * 4 + lax.rem(x + k, 4), tm)

    def at_y(k):
        return (zh * 16 + lax.rem(y + k, 4) * 4 + x, tm)

    def remote(src, dst, ss, rs, device):
        return pltpu.make_async_remote_copy(
            src_ref=src, dst_ref=dst, send_sem=ss, recv_sem=rs, device_id=device, device_id_type=MESH
        )

    def column(o):
        peer = lax.rem(here + o, 16)
        return peer // 8, lax.rem(peer, 8)

    def send(*a):
        remote(*a).start()

    def landed(ref, sem):
        pltpu.make_async_copy(ref, ref, sem).wait()

    barrier = pltpu.get_barrier_semaphore()
    for o in range(1, 16):
        h, t = column(o)
        pl.semaphore_signal(barrier, inc=1, device_id=at_z(h, t), device_id_type=MESH)
    for k in range(1, 4):
        pl.semaphore_signal(barrier, inc=1, device_id=at_x(k), device_id_type=MESH)
        pl.semaphore_signal(barrier, inc=1, device_id=at_y(k), device_id_type=MESH)

    loads = [
        pltpu.make_async_copy(src, dst, in_sem.at[n])
        for n, (src, dst) in enumerate(
            ((f_hbm, f_v), (ph_hbm, ph_v), (sq_hbm, sq_v), (p_hbm, p_v), (tw_hbm, tw_v))
        )
    ]
    for load in loads:
        load.start()

    loads[0].wait()
    for b in range(8):
        value = jnp.concatenate([f_v[pl.ds(2 * b + c, 8, stride=16), :] for c in range(2)], axis=0)
        high, low = split(value)
        s_hi[b] = high
        s_lo[b] = low
    a1[here] = s_hi[tm]
    lo[tm] = s_lo[tm]

    pl.semaphore_wait(barrier, 21)
    for o in (8, 7, 9, 6, 10, 5, 11, 4, 12, 3, 13, 2, 14, 1, 15):
        h, t = column(o)
        send(s_hi.at[t], a1.at[here], out_sem.at[0], a1r.at[tm], at_z(h, t))


    loads[1].wait()
    lane = lax.broadcasted_iota(jnp.int32, (8, 128), 1)
    sub = lax.broadcasted_iota(jnp.int32, (8, 128), 0)
    chosen = lax.rem(lane, 8) == sub
    rows = []
    for k in range(8):
        spread = jnp.where(chosen, jnp.broadcast_to(ph_v[k : k + 1, :], (8, 128)), 0.0)
        first, rest = split(spread)
        second = rest.astype(F32)
        third = spread - first.astype(F32) - second
        rows += [first.astype(F32), second, third]
    gather_lane = lax.broadcasted_iota(jnp.int32, (128, 128), 0) // 8
    gather = (gather_lane == lax.broadcasted_iota(jnp.int32, (128, 128), 1)).astype(F32).astype(BF16)
    packed = dot(jnp.concatenate(rows, axis=0).astype(BF16), gather)
    angle = jnp.zeros((8, 128), F32)
    for k in range(8):
        part = packed[24 * k : 24 * k + 8] + packed[24 * k + 8 : 24 * k + 16] + packed[24 * k + 16 : 24 * k + 24]
        angle = angle + (part if k == 0 else pltpu.roll(part, 16 * k, 1))
    cs_s[0:8, :] = jnp.cos(angle)
    cs_s[8:16, :] = jnp.sin(angle)
    mine = pl.ds(pl.multiple_of(here * 16, 16), 16)
    cs_r[mine, :] = cs_s[...]

    for n in range(2, 5):
        loads[n].wait()
    for n in range(2048 // TILE):
        block = p_v[n * TILE : (n + 1) * TILE, :]
        pm_v[n] = dot(block, sq_v[0]).astype(BF16)
        pt_v[n] = dot(sq_v[0], block, ((0,), (1,))).astype(BF16)

    for o in range(1, 8):
        t = lax.rem(tm + o, 8)
        send(s_lo.at[t], lo.at[tm], out_sem.at[1], lor.at[0], at_z(zh, t))
    for o in range(1, 16):
        h, t = column(o)
        send(cs_s, cs_r.at[mine], out_sem.at[2], csr.at[0], at_z(h, t))

    blocks = [lax.rem(zl + step, 4) * 2 + lax.rem(core + c, 2) for step, c in SLOTS]

    def first_leg(n):
        a = blocks[n]
        landed(a1.at[pl.ds(0, 1 if SLOTS[n] == (0, 0) else 2)], a1r.at[a])
        first, second = a1[a].astype(F32), a1[8 + a].astype(F32)
        for c in range(2):
            both = jnp.concatenate([first[8 * c : 8 * c + 8], second[8 * c : 8 * c + 8]], axis=0)
            mbuf[a, c, y, x] = both.astype(BF16)
        piece = mbuf.at[a, :, y, x]
        for k in range(1, 4):
            send(piece, piece, out_sem.at[3], a2r.at[n, 0], at_x(k) if n % 2 == 0 else at_y(k))

    def second_leg(n):
        a = blocks[n]
        landed(kr2.at[n], a2r.at[n, 0])
        piece = mbuf.at[a, :, y] if n % 2 == 0 else mbuf.at[a, :, :, x]
        for k in range(1, 4):
            send(piece, piece, out_sem.at[4], a2r.at[n, 1], at_y(k) if n % 2 == 0 else at_x(k))

    def compute(n):
        a = blocks[n]
        landed(kr1.at[n], a2r.at[n, 1])
        fields = jnp.concatenate([mbuf[a, c].reshape(256, 128) for c in range(2)], axis=1)
        total = None
        for t in range(2048 // TILE):
            spatial = dot(pm_v[t], fields)
            re, im = spatial[:, :128], spatial[:, 128:]
            power = re * re + im * im
            nonlin = jnp.concatenate([power * re, power * im], axis=1).astype(BF16)
            part = dot(pt_v[t], nonlin)
            total = part if total is None else total + part
        for c in range(2):
            half = total[:, 128 * c : 128 * c + 128].reshape(4, 4, 16, 128)
            kf[n, c] = half
            ks[n, c] = half.astype(BF16)
        for k in range(1, 4):
            if n % 2 == 0:
                piece, to = ks.at[n, :, :, lax.rem(x + k, 4)], at_x(k)
            else:
                piece, to = ks.at[n, :, lax.rem(y + k, 4)], at_y(k)
            send(piece, kr1.at[n, k - 1], out_sem.at[5], c1r.at[n, 0], to)

    def reduce_first(n):
        landed(kr1.at[n], c1r.at[n, 0])
        total = kf[n, :, :, x] if n % 2 == 0 else kf[n, :, y]
        for k in range(3):
            total = total + kr1[n, k].astype(F32)
        kmid[n] = total
        k1s[n] = total.astype(BF16)
        for k in range(1, 4):
            if n % 2 == 0:
                piece, to = k1s.at[n, :, lax.rem(y + k, 4)], at_y(k)
            else:
                piece, to = k1s.at[n, :, lax.rem(x + k, 4)], at_x(k)
            send(piece, kr2.at[n, k - 1], out_sem.at[6], c1r.at[n, 1], to)

    def reduce_second(n):
        landed(kr2.at[n], c1r.at[n, 1])
        total = kmid[n, :, y] if n % 2 == 0 else kmid[n, :, x]
        for k in range(3):
            total = total + kr2[n, k].astype(F32)
        kx[blocks[n]] = total

    for n in range(8):
        first_leg(n)
    for n in range(6):
        second_leg(n)
    for n in range(8):
        compute(n)
        if n < 2:
            second_leg(n + 6)
        if n >= 4:
            reduce_first(n - 4)
    for n in range(4):
        reduce_second(n)
        reduce_first(n + 4)
    for n in range(4, 8):
        reduce_second(n)

    landed(lo.at[pl.ds(0, 7)], lor.at[0])
    landed(cs_r.at[pl.ds(0, 240)], csr.at[0])
    scale = 1.0 / math.sqrt(65536.0)
    at_low = jnp.where(zh == 0, 1.0, 0.0).astype(F32)
    at_high = 1.0 - at_low
    step_re, step_im = [], []
    for a in range(8):
        own = a1[zh * 8 + a].astype(F32) + lo[a].astype(F32)
        own_re = jnp.concatenate([own[:8] * at_low, own[:8] * at_high], axis=0)
        own_im = jnp.concatenate([own[8:] * at_low, own[8:] * at_high], axis=0)
        step_re.append(own_re - kx[a, 1] * scale)
        step_im.append(own_im + kx[a, 0] * scale)
    fre, fim = fft8(step_re, step_im, -1)
    turned = []
    for r in range(8):
        cos, sin = tw_v[r : r + 1, :], tw_v[8 + r : 9 + r, :]
        turned.append(jnp.concatenate([fre[r] * cos + fim[r] * sin, fim[r] * cos - fre[r] * sin], axis=1))
    high, low = split(jnp.concatenate(turned, axis=0))
    freq = dot(high, sq_v[1]) + dot(low, sq_v[1]) + dot(high, sq_v[2])
    spun = []
    for r in range(8):
        cos, sin = cs_r[pl.ds(r, 16, stride=16), :], cs_r[pl.ds(8 + r, 16, stride=16), :]
        re, im = freq[16 * r : 16 * r + 16, :128], freq[16 * r : 16 * r + 16, 128:]
        spun.append(jnp.concatenate([re * cos - im * sin, re * sin + im * cos], axis=1))
    high, low = split(jnp.concatenate(spun, axis=0))
    back_dims = ((1,), (1,))
    back = dot(high, sq_v[1], back_dims) + dot(low, sq_v[1], back_dims) + dot(high, sq_v[2], back_dims)
    again_re, again_im = [], []
    for r in range(8):
        cos, sin = tw_v[r : r + 1, :] * (1.0 / 1024.0), tw_v[8 + r : 9 + r, :] * (1.0 / 1024.0)
        re, im = back[16 * r : 16 * r + 16, :128], back[16 * r : 16 * r + 16, 128:]
        again_re.append(re * cos - im * sin)
        again_im.append(im * cos + re * sin)
    out_re, out_im = fft8(again_re, again_im, 1)

    for a in range(8):
        low_half = jnp.concatenate([out_re[a][:8], out_im[a][:8]], axis=0)
        high_half = jnp.concatenate([out_re[a][8:], out_im[a][8:]], axis=0)
        esf[a] = low_half * at_low + high_half * at_high
        esb[a] = (low_half * at_high + high_half * at_low).astype(BF16)
    for o in range(8):
        t = lax.rem(tm + o, 8)
        send(esb.at[t], erb.at[tm], out_sem.at[7], e_sem.at[0], at_z(other, t))
    for o in range(1, 8):
        t = lax.rem(tm + o, 8)
        send(esf.at[t], erf.at[tm], out_sem.at[8], e_sem.at[1], at_z(zh, t))
    erf[tm] = esf[tm]
    landed(erb, e_sem.at[0])
    landed(erf.at[pl.ds(0, 7)], e_sem.at[1])
    for b in range(8):
        value = erf[b] + erb[b].astype(F32)
        for c in range(2):
            o_ref[pl.ds(2 * b + c, 8, stride=16), :] = value[8 * c : 8 * c + 8]
    landed(a1.at[pl.ds(0, 15)], out_sem.at[0])
    landed(lo.at[pl.ds(0, 7)], out_sem.at[1])
    landed(cs_r.at[pl.ds(0, 240)], out_sem.at[2])
    landed(kr2, out_sem.at[3])
    landed(kr1, out_sem.at[4])
    landed(kr1, out_sem.at[5])
    landed(kr2, out_sem.at[6])
    landed(erb, out_sem.at[7])
    landed(erf.at[pl.ds(0, 7)], out_sem.at[8])


def body(fields, profiles, phase):
    square, twist = tables()
    dma = pltpu.SemaphoreType.DMA
    hbm_spec = pl.BlockSpec(memory_space=pltpu.HBM)
    out = pl.pallas_call(
        kernel,
        out_shape=jax.ShapeDtypeStruct((128, 128), F32),
        in_specs=[hbm_spec] * 5,
        out_specs=pl.BlockSpec(memory_space=pltpu.VMEM),
        scratch_shapes=[
            pltpu.VMEM((128, 128), F32),
            pltpu.VMEM((2048, 256), BF16),
            pltpu.VMEM((8, 128), F32),
            pltpu.VMEM((3, 256, 256), BF16),
            pltpu.VMEM((16, 128), F32),
            pltpu.VMEM((2048 // TILE, TILE, 256), BF16),
            pltpu.VMEM((2048 // TILE, 256, TILE), BF16),
            pltpu.VMEM((8, 2, 4, 4, 16, 128), BF16),
            pltpu.VMEM((8, 16, 128), BF16),
            pltpu.VMEM((8, 16, 128), BF16),
            pltpu.VMEM((16, 16, 128), BF16),
            pltpu.VMEM((8, 16, 128), BF16),
            pltpu.VMEM((16, 128), F32),
            pltpu.VMEM((256, 128), F32),
            pltpu.VMEM((8, 2, 4, 4, 16, 128), F32),
            pltpu.VMEM((8, 2, 4, 4, 16, 128), BF16),
            pltpu.VMEM((8, 3, 2, 4, 16, 128), BF16),
            pltpu.VMEM((8, 2, 4, 16, 128), BF16),
            pltpu.VMEM((8, 3, 2, 16, 128), BF16),
            pltpu.VMEM((8, 2, 4, 16, 128), F32),
            pltpu.VMEM((8, 2, 16, 128), F32),
            pltpu.VMEM((8, 16, 128), F32),
            pltpu.VMEM((8, 16, 128), BF16),
            pltpu.VMEM((8, 16, 128), F32),
            pltpu.VMEM((8, 16, 128), BF16),
            dma((5,)), dma((9,)), dma((8,)), dma((1,)), dma((1,)), dma((8, 2)), dma((8, 2)), dma((2,)),
        ],
        compiler_params=pltpu.CompilerParams(
            collective_id=0, has_side_effects=True, vmem_limit_bytes=67_043_328
        ),
    )(fields.reshape(128, 128), profiles, phase.reshape(8, 128), jnp.asarray(square), jnp.asarray(twist))
    return out.reshape(8, 8, 2, 128)


def solution(mesh):
    return jax.shard_map(
        body,
        mesh=mesh,
        in_specs=(P("pix", None, None, "tm"), P("pix", None), P(("pix", "tm"), None)),
        out_specs=P("pix", None, None, "tm"),
        check_vma=False,
    )
```

```python
import functools
import math

import jax
import jax.numpy as jnp
import numpy as np
from jax import lax
from jax.experimental import pallas as pl
from jax.experimental.pallas import tpu as pltpu
from jax.sharding import PartitionSpec as P

MESH = pl.DeviceIdType.MESH
F32 = jnp.float32
BF16 = jnp.bfloat16

SLOTS = ((2, 0), (2, 1), (1, 0), (1, 1), (3, 0), (3, 1), (0, 1), (0, 0))
TILE = 256
STRAIGHT_IN = (0, 1)
STRAIGHT_OUT = (7,)
GROUPS = ((0,), (1,), (2,), (3,), (4,), (5,), (6,), (7,))
FIRST_ORDER = (2, 3, 0, 1, 4, 5, 6, 7)
EARLY, FIRST_LAG = 2, 4
FAR_FIRST = (10, 6, 9, 11, 14, 2, 5, 7, 8, 13, 15, 1, 3, 4, 12)


def tables():
    row = np.arange(256)
    order = (row // 8 % 2) * 128 + (row // 16) * 8 + row % 8
    perm = np.zeros((256, 256), np.float32)
    perm[order, row] = 1.0
    angle = 2.0 * np.pi * (np.outer(np.arange(128), np.arange(128)) % 128) / 128.0
    cos, sin = np.cos(angle), np.sin(angle)
    dft = np.block([[cos, -sin], [sin, cos]]).astype(np.float32)
    high = dft.astype(jnp.bfloat16)
    low = (dft - high.astype(np.float32)).astype(jnp.bfloat16)
    turn = 2.0 * np.pi * np.outer(np.arange(8), np.arange(128)) / 1024.0
    twist = np.concatenate([np.cos(turn), np.sin(turn)]).astype(np.float32)
    square = np.stack([perm.astype(jnp.bfloat16), high, low])
    return square, twist


def fft8(re, im, sign):
    half = math.sqrt(0.5)

    def turned(x, y, k):
        if k == 0:
            return x, y
        if k == 1:
            return (x - sign * y) * half, (y + sign * x) * half
        if k == 2:
            return (-y, x) if sign > 0 else (y, -x)
        return (-x - sign * y) * half, (-y + sign * x) * half

    def four(r, i):
        ar, ai, br, bi = r[0] + r[2], i[0] + i[2], r[0] - r[2], i[0] - i[2]
        cr, ci, dr, di = r[1] + r[3], i[1] + i[3], r[1] - r[3], i[1] - i[3]
        dr, di = turned(dr, di, 2)
        return [ar + cr, br + dr, ar - cr, br - dr], [ai + ci, bi + di, ai - ci, bi - di]

    er, ei = four(re[0::2], im[0::2])
    od, oi = four(re[1::2], im[1::2])
    out_re, out_im = [None] * 8, [None] * 8
    for k in range(4):
        tr, ti = turned(od[k], oi[k], k)
        out_re[k], out_im[k] = er[k] + tr, ei[k] + ti
        out_re[k + 4], out_im[k + 4] = er[k] - tr, ei[k] - ti
    return out_re, out_im


def split(value):
    high = value.astype(BF16)
    return high, (value - high.astype(F32)).astype(BF16)


def dot(a, b, dims=((1,), (0,))):
    return lax.dot_general(a, b, (dims, ((), ())), preferred_element_type=F32)


def kernel(
    f_hbm, p_hbm, ph_hbm, sq_hbm, tw_hbm, o_ref,
    f_v, p_v, ph_v, sq_v, tw_v, pm_v, pt_v, mbuf, s_hi, s_lo, a1, lo, cs_s, cs_r,
    tile, kf, ks, krd, kr1, k1s, kr2, kmid, kx, esf, esb, erf, erb,
    in_sem, out_sem, a1r, lor, csr, a2r, c1r, e_sem,
):
    pix, tm = lax.axis_index("pix"), lax.axis_index("tm")
    zh, y, x = pix // 16, (pix // 4) % 4, pix % 4
    yx = pix % 16
    zl, core = tm // 2, tm % 2
    other = 1 - zh
    here = zh * 8 + tm

    def at_z(h, t):
        return (h * 16 + yx, t)

    def at_x(k):
        return (zh * 16 + y * 4 + lax.rem(x + k, 4), tm)

    def at_y(k):
        return (zh * 16 + lax.rem(y + k, 4) * 4 + x, tm)

    def remote(src, dst, ss, rs, device):
        return pltpu.make_async_remote_copy(
            src_ref=src, dst_ref=dst, send_sem=ss, recv_sem=rs, device_id=device, device_id_type=MESH
        )

    def at_plane(k):
        to_y, to_x = lax.rem(y + k // 4, 4), lax.rem(x + k % 4, 4)
        return to_y, to_x, (zh * 16 + to_y * 4 + to_x, tm)

    def column(o):
        peer = lax.rem(here + o, 16)
        return peer // 8, lax.rem(peer, 8)

    sent = [0] * 4

    def send(src, dst, phase, rs, device):
        remote(src, dst, out_sem.at[phase], rs, device).start()
        sent[phase] += math.prod(src.shape) * src.dtype.itemsize // 4096

    def landed(tiles, sem):
        ref = tile.at[pl.ds(0, tiles)]
        pltpu.make_async_copy(ref, ref, sem).wait()

    barrier = pltpu.get_barrier_semaphore()
    for o in range(1, 16):
        h, t = column(o)
        pl.semaphore_signal(barrier, inc=1, device_id=at_z(h, t), device_id_type=MESH)
    for k in range(1, 16):
        pl.semaphore_signal(barrier, inc=1, device_id=at_plane(k)[2], device_id_type=MESH)

    loads = [
        pltpu.make_async_copy(src, dst, in_sem.at[n])
        for n, (src, dst) in enumerate(
            ((f_hbm, f_v), (ph_hbm, ph_v), (sq_hbm, sq_v), (p_hbm, p_v), (tw_hbm, tw_v))
        )
    ]
    for load in loads:
        load.start()

    loads[0].wait()
    for b in range(8):
        value = jnp.concatenate([f_v[pl.ds(2 * b + c, 8, stride=16), :] for c in range(2)], axis=0)
        high, low = split(value)
        s_hi[b] = high
        s_lo[b] = low
    a1[here] = s_hi[tm]
    lo[tm] = s_lo[tm]

    pl.semaphore_wait(barrier, 30)
    for o in (8, 7, 9, 6, 10, 5, 11, 4, 12, 3, 13, 2, 14, 1, 15):
        h, t = column(o)
        send(s_hi.at[t], a1.at[here], 0, a1r.at[tm], at_z(h, t))


    loads[1].wait()
    lane = lax.broadcasted_iota(jnp.int32, (8, 128), 1)
    sub = lax.broadcasted_iota(jnp.int32, (8, 128), 0)
    chosen = lax.rem(lane, 8) == sub
    rows = []
    for k in range(8):
        spread = jnp.where(chosen, jnp.broadcast_to(ph_v[k : k + 1, :], (8, 128)), 0.0)
        first, rest = split(spread)
        second = rest.astype(F32)
        third = spread - first.astype(F32) - second
        rows += [first.astype(F32), second, third]
    gather_lane = lax.broadcasted_iota(jnp.int32, (128, 128), 0) // 8
    gather = (gather_lane == lax.broadcasted_iota(jnp.int32, (128, 128), 1)).astype(F32).astype(BF16)
    packed = dot(jnp.concatenate(rows, axis=0).astype(BF16), gather)
    angle = jnp.zeros((8, 128), F32)
    for k in range(8):
        part = packed[24 * k : 24 * k + 8] + packed[24 * k + 8 : 24 * k + 16] + packed[24 * k + 16 : 24 * k + 24]
        angle = angle + (part if k == 0 else pltpu.roll(part, 16 * k, 1))
    cs_s[0:8, :] = jnp.cos(angle)
    cs_s[8:16, :] = jnp.sin(angle)
    mine = pl.ds(pl.multiple_of(here * 16, 16), 16)
    cs_r[mine, :] = cs_s[...]

    for n in range(2, 5):
        loads[n].wait()
    for n in range(2048 // TILE):
        block = p_v[n * TILE : (n + 1) * TILE, :]
        pm_v[n] = dot(block, sq_v[0]).astype(BF16)
        pt_v[n] = dot(sq_v[0], block, ((0,), (1,))).astype(BF16)

    blocks = [lax.rem(zl + step, 4) * 2 + lax.rem(core + c, 2) for step, c in SLOTS]

    def first_leg(n):
        a = blocks[n]
        landed(1 if SLOTS[n] == (0, 0) else 2, a1r.at[a])
        first, second = a1[a].astype(F32), a1[8 + a].astype(F32)
        for c in range(2):
            both = jnp.concatenate([first[8 * c : 8 * c + 8], second[8 * c : 8 * c + 8]], axis=0)
            mbuf[a, c, y, x] = both.astype(BF16)
        piece = mbuf.at[a, :, y, x]
        if n in STRAIGHT_IN:
            for k in FAR_FIRST:
                send(piece, piece, 1, a2r.at[n, 1], at_plane(k)[2])
            return
        for k in range(1, 4):
            send(piece, piece, 1, a2r.at[n, 0], at_x(k) if n % 2 == 0 else at_y(k))

    def second_leg(n):
        a = blocks[n]
        landed(6, a2r.at[n, 0])
        piece = mbuf.at[a, :, y] if n % 2 == 0 else mbuf.at[a, :, :, x]
        for k in (2, 1, 3):
            send(piece, piece, 1, a2r.at[n, 1], at_y(k) if n % 2 == 0 else at_x(k))

    def spread(n, total):
        for c in range(2):
            half = total[:, 128 * c : 128 * c + 128].reshape(4, 4, 16, 128)
            kf[n, c] = half
            ks[n, c] = half.astype(BF16)
        if n in STRAIGHT_OUT:
            for k in FAR_FIRST:
                to_y, to_x, to = at_plane(k)
                send(ks.at[n, :, to_y, to_x], krd.at[STRAIGHT_OUT.index(n), k - 1], 2, c1r.at[n, 0], to)
            return
        for k in (2, 1, 3):
            if n % 2 == 0:
                piece, to = ks.at[n, :, :, lax.rem(x + k, 4)], at_x(k)
            else:
                piece, to = ks.at[n, :, lax.rem(y + k, 4)], at_y(k)
            send(piece, kr1.at[n, k - 1], 2, c1r.at[n, 0], to)

    def compute(slots):
        pieces = []
        for n in slots:
            landed(30 if n in STRAIGHT_IN else 24, a2r.at[n, 1])
            pieces += [mbuf[blocks[n], c].reshape(256, 128) for c in range(2)]
        fields = jnp.concatenate(pieces, axis=1)
        total = None
        for t in range(2048 // TILE):
            spatial = dot(pm_v[t], fields)
            cubes = []
            for at in range(0, 256 * len(slots), 256):
                re, im = spatial[:, at : at + 128], spatial[:, at + 128 : at + 256]
                power = re * re + im * im
                cubes += [power * re, power * im]
            part = dot(pt_v[t], jnp.concatenate(cubes, axis=1).astype(BF16))
            total = part if total is None else total + part
        for at, n in enumerate(slots):
            spread(n, total[:, 256 * at : 256 * at + 256])

    def reduce_first(n):
        landed(24, c1r.at[n, 0])
        total = kf[n, :, :, x] if n % 2 == 0 else kf[n, :, y]
        for k in range(3):
            total = total + kr1[n, k].astype(F32)
        kmid[n] = total
        k1s[n] = total.astype(BF16)
        for k in range(1, 4):
            if n % 2 == 0:
                piece, to = k1s.at[n, :, lax.rem(y + k, 4)], at_y(k)
            else:
                piece, to = k1s.at[n, :, lax.rem(x + k, 4)], at_x(k)
            send(piece, kr2.at[n, k - 1], 2, c1r.at[n, 1], to)

    def reduce_straight(n):
        landed(30, c1r.at[n, 0])
        total = kf[n, :, y, x]
        for k in range(15):
            total = total + krd[STRAIGHT_OUT.index(n), k].astype(F32)
        kx[blocks[n]] = total

    def reduce_second(n):
        landed(6, c1r.at[n, 1])
        total = kmid[n, :, y] if n % 2 == 0 else kmid[n, :, x]
        for k in range(3):
            total = total + kr2[n, k].astype(F32)
        kx[blocks[n]] = total

    for n in FIRST_ORDER:
        first_leg(n)
    for o in range(1, 8):
        t = lax.rem(tm + o, 8)
        send(s_lo.at[t], lo.at[tm], 0, lor.at[0], at_z(zh, t))
    for o in range(1, 16):
        h, t = column(o)
        send(cs_s, cs_r.at[mine], 0, csr.at[0], at_z(h, t))
    two_legs = [n for n in range(8) if n not in STRAIGHT_IN]
    out_legs = [n for n in range(8) if n not in STRAIGHT_OUT]
    for n in two_legs[:EARLY]:
        second_leg(n)
    for slots in GROUPS:
        compute(slots)
        if slots[0] == 0:
            for m in two_legs[EARLY:]:
                second_leg(m)
        for m in out_legs:
            if m + FIRST_LAG in slots:
                reduce_first(m)
    for m in out_legs:
        if m + FIRST_LAG > 7:
            reduce_first(m)
    for m in out_legs:
        reduce_second(m)
    for m in STRAIGHT_OUT:
        reduce_straight(m)

    landed(7, lor.at[0])
    landed(30, csr.at[0])
    scale = 1.0 / math.sqrt(65536.0)
    at_low = jnp.where(zh == 0, 1.0, 0.0).astype(F32)
    at_high = 1.0 - at_low
    step_re, step_im = [], []
    for a in range(8):
        own = a1[zh * 8 + a].astype(F32) + lo[a].astype(F32)
        own_re = jnp.concatenate([own[:8] * at_low, own[:8] * at_high], axis=0)
        own_im = jnp.concatenate([own[8:] * at_low, own[8:] * at_high], axis=0)
        step_re.append(own_re - kx[a, 1] * scale)
        step_im.append(own_im + kx[a, 0] * scale)
    fre, fim = fft8(step_re, step_im, -1)
    turned = []
    for r in range(8):
        cos, sin = tw_v[r : r + 1, :], tw_v[8 + r : 9 + r, :]
        turned.append(jnp.concatenate([fre[r] * cos + fim[r] * sin, fim[r] * cos - fre[r] * sin], axis=1))
    high, low = split(jnp.concatenate(turned, axis=0))
    freq = dot(high, sq_v[1]) + dot(low, sq_v[1]) + dot(high, sq_v[2])
    spun = []
    for r in range(8):
        cos, sin = cs_r[pl.ds(r, 16, stride=16), :], cs_r[pl.ds(8 + r, 16, stride=16), :]
        re, im = freq[16 * r : 16 * r + 16, :128], freq[16 * r : 16 * r + 16, 128:]
        spun.append(jnp.concatenate([re * cos - im * sin, re * sin + im * cos], axis=1))
    high, low = split(jnp.concatenate(spun, axis=0))
    back_dims = ((1,), (1,))
    back = dot(high, sq_v[1], back_dims) + dot(low, sq_v[1], back_dims) + dot(high, sq_v[2], back_dims)
    again_re, again_im = [], []
    for r in range(8):
        cos, sin = tw_v[r : r + 1, :] * (1.0 / 1024.0), tw_v[8 + r : 9 + r, :] * (1.0 / 1024.0)
        re, im = back[16 * r : 16 * r + 16, :128], back[16 * r : 16 * r + 16, 128:]
        again_re.append(re * cos - im * sin)
        again_im.append(im * cos + re * sin)
    out_re, out_im = fft8(again_re, again_im, 1)

    for a in range(8):
        low_half = jnp.concatenate([out_re[a][:8], out_im[a][:8]], axis=0)
        high_half = jnp.concatenate([out_re[a][8:], out_im[a][8:]], axis=0)
        esf[a] = (low_half * at_low + high_half * at_high).astype(BF16)
        esb[a] = (low_half * at_high + high_half * at_low).astype(BF16)
    for o in range(8):
        t = lax.rem(tm + o, 8)
        send(esb.at[t], erb.at[tm], 3, e_sem.at[0], at_z(other, t))
    for o in range(1, 8):
        t = lax.rem(tm + o, 8)
        send(esf.at[t], erf.at[tm], 3, e_sem.at[1], at_z(zh, t))
    erf[tm] = esf[tm]
    landed(8, e_sem.at[0])
    landed(7, e_sem.at[1])
    for b in range(8):
        value = erf[b].astype(F32) + erb[b].astype(F32)
        for c in range(2):
            o_ref[pl.ds(2 * b + c, 8, stride=16), :] = value[8 * c : 8 * c + 8]
    for phase in range(4):
        landed(sent[phase], out_sem.at[phase])


def body(fields, profiles, phase):
    square, twist = tables()
    dma = pltpu.SemaphoreType.DMA
    hbm_spec = pl.BlockSpec(memory_space=pltpu.HBM)
    out = pl.pallas_call(
        kernel,
        out_shape=jax.ShapeDtypeStruct((128, 128), F32),
        in_specs=[hbm_spec] * 5,
        out_specs=pl.BlockSpec(memory_space=pltpu.VMEM),
        scratch_shapes=[
            pltpu.VMEM((128, 128), F32),
            pltpu.VMEM((2048, 256), BF16),
            pltpu.VMEM((8, 128), F32),
            pltpu.VMEM((3, 256, 256), BF16),
            pltpu.VMEM((16, 128), F32),
            pltpu.VMEM((2048 // TILE, TILE, 256), BF16),
            pltpu.VMEM((2048 // TILE, 256, TILE), BF16),
            pltpu.VMEM((8, 2, 4, 4, 16, 128), BF16),
            pltpu.VMEM((8, 16, 128), BF16),
            pltpu.VMEM((8, 16, 128), BF16),
            pltpu.VMEM((16, 16, 128), BF16),
            pltpu.VMEM((8, 16, 128), BF16),
            pltpu.VMEM((16, 128), F32),
            pltpu.VMEM((256, 128), F32),
            pltpu.VMEM((512, 16, 128), BF16),
            pltpu.VMEM((8, 2, 4, 4, 16, 128), F32),
            pltpu.VMEM((8, 2, 4, 4, 16, 128), BF16),
            pltpu.VMEM((len(STRAIGHT_OUT), 15, 2, 16, 128), BF16),
            pltpu.VMEM((8, 3, 2, 4, 16, 128), BF16),
            pltpu.VMEM((8, 2, 4, 16, 128), BF16),
            pltpu.VMEM((8, 3, 2, 16, 128), BF16),
            pltpu.VMEM((8, 2, 4, 16, 128), F32),
            pltpu.VMEM((8, 2, 16, 128), F32),
            pltpu.VMEM((8, 16, 128), BF16),
            pltpu.VMEM((8, 16, 128), BF16),
            pltpu.VMEM((8, 16, 128), BF16),
            pltpu.VMEM((8, 16, 128), BF16),
            dma((5,)), dma((4,)), dma((8,)), dma((1,)), dma((1,)), dma((8, 2)), dma((8, 2)), dma((2,)),
        ],
        compiler_params=pltpu.CompilerParams(
            collective_id=0, has_side_effects=True, vmem_limit_bytes=44_000_000
        ),
    )(*[pltpu.with_memory_space_constraint(v, pltpu.HBM) for v in (fields.reshape(128, 128), profiles, phase.reshape(8, 128), jnp.asarray(square), jnp.asarray(twist))])
    return out.reshape(8, 8, 2, 128)


def solution(mesh):
    return jax.shard_map(
        body,
        mesh=mesh,
        in_specs=(P("pix", None, None, "tm"), P("pix", None), P(("pix", "tm"), None)),
        out_specs=P("pix", None, None, "tm"),
        check_vma=False,
    )
```

```python
import functools
import math

import jax
import jax.numpy as jnp
import numpy as np
from jax import lax
from jax.experimental import pallas as pl
from jax.experimental.pallas import tpu as pltpu
from jax.sharding import PartitionSpec as P

MESH = pl.DeviceIdType.MESH
F32 = jnp.float32
BF16 = jnp.bfloat16

SLOTS = ((2, 1), (2, 0), (1, 1), (1, 0), (3, 1), (3, 0), (0, 1), (0, 0))
TILE = 256
STRAIGHT_IN = (0, 1)
STRAIGHT_OUT = (6, 7)
GROUPS = ((0,), (1,), (2,), (3,), (4,), (5,), (6,), (7,))
FIRST_ORDER = (2, 0, 4, 3, 1, 5, 6, 7)
EARLY, FIRST_LAG = 2, 4
FAR_FIRST = (10, 6, 9, 11, 14, 2, 5, 7, 8, 13, 15, 1, 3, 4, 12)


def tables():
    row = np.arange(256)
    order = (row // 8 % 2) * 128 + (row // 16) * 8 + row % 8
    perm = np.zeros((256, 256), np.float32)
    perm[order, row] = 1.0
    angle = 2.0 * np.pi * (np.outer(np.arange(128), np.arange(128)) % 128) / 128.0
    cos, sin = np.cos(angle), np.sin(angle)
    dft = np.block([[cos, -sin], [sin, cos]]).astype(np.float32)
    high = dft.astype(jnp.bfloat16)
    low = (dft - high.astype(np.float32)).astype(jnp.bfloat16)
    turn = 2.0 * np.pi * np.outer(np.arange(8), np.arange(128)) / 1024.0
    twist = np.concatenate([np.cos(turn), np.sin(turn)]).astype(np.float32)
    square = np.stack([perm.astype(jnp.bfloat16), high, low])
    return square, twist


def fft8(re, im, sign):
    half = math.sqrt(0.5)

    def turned(x, y, k):
        if k == 0:
            return x, y
        if k == 1:
            return (x - sign * y) * half, (y + sign * x) * half
        if k == 2:
            return (-y, x) if sign > 0 else (y, -x)
        return (-x - sign * y) * half, (-y + sign * x) * half

    def four(r, i):
        ar, ai, br, bi = r[0] + r[2], i[0] + i[2], r[0] - r[2], i[0] - i[2]
        cr, ci, dr, di = r[1] + r[3], i[1] + i[3], r[1] - r[3], i[1] - i[3]
        dr, di = turned(dr, di, 2)
        return [ar + cr, br + dr, ar - cr, br - dr], [ai + ci, bi + di, ai - ci, bi - di]

    er, ei = four(re[0::2], im[0::2])
    od, oi = four(re[1::2], im[1::2])
    out_re, out_im = [None] * 8, [None] * 8
    for k in range(4):
        tr, ti = turned(od[k], oi[k], k)
        out_re[k], out_im[k] = er[k] + tr, ei[k] + ti
        out_re[k + 4], out_im[k + 4] = er[k] - tr, ei[k] - ti
    return out_re, out_im


def split(value):
    high = value.astype(BF16)
    return high, (value - high.astype(F32)).astype(BF16)


def dot(a, b, dims=((1,), (0,))):
    return lax.dot_general(a, b, (dims, ((), ())), preferred_element_type=F32)


def kernel(
    f_hbm, p_hbm, ph_hbm, sq_hbm, tw_hbm, o_ref,
    f_v, p_v, ph_v, sq_v, tw_v, pm_v, pt_v, mbuf, s_hi, s_lo, a1, lo, cs_s, cs_r,
    tile, kf, ks, krd, kr1, k1s, kr2, kmid, kx, esf, esb, erf, erb,
    in_sem, out_sem, a1r, lor, csr, a2r, c1r, e_sem,
):
    pix, tm = lax.axis_index("pix"), lax.axis_index("tm")
    zh, y, x = pix // 16, (pix // 4) % 4, pix % 4
    yx = pix % 16
    zl, core = tm // 2, tm % 2
    other = 1 - zh
    here = zh * 8 + tm

    def at_z(h, t):
        return (h * 16 + yx, t)

    def at_x(k):
        return (zh * 16 + y * 4 + lax.rem(x + k, 4), tm)

    def at_y(k):
        return (zh * 16 + lax.rem(y + k, 4) * 4 + x, tm)

    def remote(src, dst, ss, rs, device):
        return pltpu.make_async_remote_copy(
            src_ref=src, dst_ref=dst, send_sem=ss, recv_sem=rs, device_id=device, device_id_type=MESH
        )

    def at_plane(k):
        to_y, to_x = lax.rem(y + k // 4, 4), lax.rem(x + k % 4, 4)
        return to_y, to_x, (zh * 16 + to_y * 4 + to_x, tm)

    def column(o):
        peer = lax.rem(here + o, 16)
        return peer // 8, lax.rem(peer, 8)

    sent = [0] * 4

    def send(src, dst, phase, rs, device):
        remote(src, dst, out_sem.at[phase], rs, device).start()
        sent[phase] += math.prod(src.shape) * src.dtype.itemsize // 4096

    def landed(tiles, sem):
        ref = tile.at[pl.ds(0, tiles)]
        pltpu.make_async_copy(ref, ref, sem).wait()

    barrier = pltpu.get_barrier_semaphore()
    for o in range(1, 16):
        h, t = column(o)
        pl.semaphore_signal(barrier, inc=1, device_id=at_z(h, t), device_id_type=MESH)
    for k in range(1, 16):
        pl.semaphore_signal(barrier, inc=1, device_id=at_plane(k)[2], device_id_type=MESH)

    loads = [
        pltpu.make_async_copy(src, dst, in_sem.at[n])
        for n, (src, dst) in enumerate(
            ((f_hbm, f_v), (ph_hbm, ph_v), (sq_hbm, sq_v), (p_hbm, p_v), (tw_hbm, tw_v))
        )
    ]
    for load in loads:
        load.start()

    loads[0].wait()
    for b in range(8):
        value = jnp.concatenate([f_v[pl.ds(2 * b + c, 8, stride=16), :] for c in range(2)], axis=0)
        high, low = split(value)
        s_hi[b] = high
        s_lo[b] = low
    a1[here] = s_hi[tm]
    lo[tm] = s_lo[tm]

    pl.semaphore_wait(barrier, 30)
    for o in (8, 7, 9, 6, 10, 5, 11, 4, 12, 3, 13, 2, 14, 1, 15):
        h, t = column(o)
        send(s_hi.at[t], a1.at[here], 0, a1r.at[tm], at_z(h, t))


    loads[1].wait()
    lane = lax.broadcasted_iota(jnp.int32, (8, 128), 1)
    sub = lax.broadcasted_iota(jnp.int32, (8, 128), 0)
    chosen = lax.rem(lane, 8) == sub
    rows = []
    for k in range(8):
        spread = jnp.where(chosen, jnp.broadcast_to(ph_v[k : k + 1, :], (8, 128)), 0.0)
        first, rest = split(spread)
        second = rest.astype(F32)
        third = spread - first.astype(F32) - second
        rows += [first.astype(F32), second, third]
    gather_lane = lax.broadcasted_iota(jnp.int32, (128, 128), 0) // 8
    gather = (gather_lane == lax.broadcasted_iota(jnp.int32, (128, 128), 1)).astype(F32).astype(BF16)
    packed = dot(jnp.concatenate(rows, axis=0).astype(BF16), gather)
    angle = jnp.zeros((8, 128), F32)
    for k in range(8):
        part = packed[24 * k : 24 * k + 8] + packed[24 * k + 8 : 24 * k + 16] + packed[24 * k + 16 : 24 * k + 24]
        angle = angle + (part if k == 0 else pltpu.roll(part, 16 * k, 1))
    cs_s[0:8, :] = jnp.cos(angle)
    cs_s[8:16, :] = jnp.sin(angle)
    mine = pl.ds(pl.multiple_of(here * 16, 16), 16)
    cs_r[mine, :] = cs_s[...]

    for n in range(2, 5):
        loads[n].wait()
    for n in range(2048 // TILE):
        block = p_v[n * TILE : (n + 1) * TILE, :]
        pm_v[n] = dot(block, sq_v[0]).astype(BF16)
        pt_v[n] = dot(sq_v[0], block, ((0,), (1,))).astype(BF16)

    blocks = [lax.rem(zl + step, 4) * 2 + c for step, c in SLOTS]

    def first_leg(n):
        a = blocks[n]
        if n < 6:
            landed(2, a1r.at[a])
        elif n == 6:
            landed(2, a1r.at[zl * 2 + 1 - core])
            landed(1, a1r.at[tm])
        first, second = a1[a].astype(F32), a1[8 + a].astype(F32)
        for c in range(2):
            both = jnp.concatenate([first[8 * c : 8 * c + 8], second[8 * c : 8 * c + 8]], axis=0)
            mbuf[a, y, x, c] = both.astype(BF16)
        piece = mbuf.at[a, y, x]
        if n in STRAIGHT_IN:
            for k in FAR_FIRST:
                send(piece, piece, 1, a2r.at[n, 1], at_plane(k)[2])
            return
        for k in range(1, 4):
            send(piece, piece, 1, a2r.at[n, 0], at_x(k) if n % 2 == 0 else at_y(k))

    def second_leg(n):
        a = blocks[n]
        landed(6, a2r.at[n, 0])
        piece = mbuf.at[a, y] if n % 2 == 0 else mbuf.at[a, :, x]
        for k in (2, 1, 3):
            send(piece, piece, 1, a2r.at[n, 1], at_y(k) if n % 2 == 0 else at_x(k))

    def spread(n, total):
        for c in range(2):
            half = total[:, 128 * c : 128 * c + 128].reshape(4, 4, 16, 128)
            kf[n, :, :, c] = half
            ks[n, :, :, c] = half.astype(BF16)
        if n in STRAIGHT_OUT:
            for k in FAR_FIRST:
                to_y, to_x, to = at_plane(k)
                send(ks.at[n, to_y, to_x], krd.at[STRAIGHT_OUT.index(n), k - 1], 2, c1r.at[n, 0], to)
            return
        for k in (2, 1, 3):
            if n % 2 == 0:
                piece, to = ks.at[n, :, lax.rem(x + k, 4)], at_x(k)
            else:
                piece, to = ks.at[n, lax.rem(y + k, 4)], at_y(k)
            send(piece, kr1.at[n, k - 1], 2, c1r.at[n, 0], to)

    def compute(slots):
        pieces = []
        for n in slots:
            landed(30 if n in STRAIGHT_IN else 24, a2r.at[n, 1])
            pieces += [mbuf[blocks[n], :, :, c].reshape(256, 128) for c in range(2)]
        fields = jnp.concatenate(pieces, axis=1)
        total = None
        for t in range(2048 // TILE):
            spatial = dot(pm_v[t], fields)
            cubes = []
            for at in range(0, 256 * len(slots), 256):
                re, im = spatial[:, at : at + 128], spatial[:, at + 128 : at + 256]
                power = re * re + im * im
                cubes += [power * re, power * im]
            part = dot(pt_v[t], jnp.concatenate(cubes, axis=1).astype(BF16))
            total = part if total is None else total + part
        for at, n in enumerate(slots):
            spread(n, total[:, 256 * at : 256 * at + 256])

    def reduce_first(n):
        landed(24, c1r.at[n, 0])
        total = kf[n, :, x] if n % 2 == 0 else kf[n, y]
        for k in range(3):
            total = total + kr1[n, k].astype(F32)
        kmid[n] = total
        k1s[n] = total.astype(BF16)
        for k in range(1, 4):
            if n % 2 == 0:
                piece, to = k1s.at[n, lax.rem(y + k, 4)], at_y(k)
            else:
                piece, to = k1s.at[n, lax.rem(x + k, 4)], at_x(k)
            send(piece, kr2.at[n, k - 1], 2, c1r.at[n, 1], to)

    def reduce_straight(n):
        landed(30, c1r.at[n, 0])
        total = kf[n, y, x]
        for k in range(15):
            total = total + krd[STRAIGHT_OUT.index(n), k].astype(F32)
        kx[blocks[n]] = total

    def reduce_second(n):
        landed(6, c1r.at[n, 1])
        total = kmid[n, y] if n % 2 == 0 else kmid[n, x]
        for k in range(3):
            total = total + kr2[n, k].astype(F32)
        kx[blocks[n]] = total

    for n in FIRST_ORDER:
        first_leg(n)
    for o in range(1, 8):
        t = lax.rem(tm + o, 8)
        send(s_lo.at[t], lo.at[tm], 0, lor.at[0], at_z(zh, t))
    for o in range(1, 16):
        h, t = column(o)
        send(cs_s, cs_r.at[mine], 0, csr.at[0], at_z(h, t))
    two_legs = [n for n in range(8) if n not in STRAIGHT_IN]
    out_legs = [n for n in range(8) if n not in STRAIGHT_OUT]
    for n in two_legs[:EARLY]:
        second_leg(n)
    for slots in GROUPS:
        compute(slots)
        if slots[0] == 0:
            for m in two_legs[EARLY:]:
                second_leg(m)
        for m in out_legs:
            if m + FIRST_LAG in slots:
                reduce_first(m)
    for m in out_legs:
        if m + FIRST_LAG > 7:
            reduce_first(m)
    for m in out_legs:
        reduce_second(m)
    for m in STRAIGHT_OUT:
        reduce_straight(m)

    landed(7, lor.at[0])
    landed(30, csr.at[0])
    scale = 1.0 / math.sqrt(65536.0)
    at_low = jnp.where(zh == 0, 1.0, 0.0).astype(F32)
    at_high = 1.0 - at_low
    step_re, step_im = [], []
    for a in range(8):
        own = a1[zh * 8 + a].astype(F32) + lo[a].astype(F32)
        own_re = jnp.concatenate([own[:8] * at_low, own[:8] * at_high], axis=0)
        own_im = jnp.concatenate([own[8:] * at_low, own[8:] * at_high], axis=0)
        step_re.append(own_re - kx[a, 1] * scale)
        step_im.append(own_im + kx[a, 0] * scale)
    fre, fim = fft8(step_re, step_im, -1)
    turned = []
    for r in range(8):
        cos, sin = tw_v[r : r + 1, :], tw_v[8 + r : 9 + r, :]
        turned.append(jnp.concatenate([fre[r] * cos + fim[r] * sin, fim[r] * cos - fre[r] * sin], axis=1))
    high, low = split(jnp.concatenate(turned, axis=0))
    freq = dot(high, sq_v[1]) + dot(low, sq_v[1]) + dot(high, sq_v[2])
    spun = []
    for r in range(8):
        cos, sin = cs_r[pl.ds(r, 16, stride=16), :], cs_r[pl.ds(8 + r, 16, stride=16), :]
        re, im = freq[16 * r : 16 * r + 16, :128], freq[16 * r : 16 * r + 16, 128:]
        spun.append(jnp.concatenate([re * cos - im * sin, re * sin + im * cos], axis=1))
    high, low = split(jnp.concatenate(spun, axis=0))
    back_dims = ((1,), (1,))
    back = dot(high, sq_v[1], back_dims) + dot(low, sq_v[1], back_dims) + dot(high, sq_v[2], back_dims)
    again_re, again_im = [], []
    for r in range(8):
        cos, sin = tw_v[r : r + 1, :] * (1.0 / 1024.0), tw_v[8 + r : 9 + r, :] * (1.0 / 1024.0)
        re, im = back[16 * r : 16 * r + 16, :128], back[16 * r : 16 * r + 16, 128:]
        again_re.append(re * cos - im * sin)
        again_im.append(im * cos + re * sin)
    out_re, out_im = fft8(again_re, again_im, 1)

    for a in range(8):
        low_half = jnp.concatenate([out_re[a][:8], out_im[a][:8]], axis=0)
        high_half = jnp.concatenate([out_re[a][8:], out_im[a][8:]], axis=0)
        esf[a] = (low_half * at_low + high_half * at_high).astype(BF16)
        esb[a] = (low_half * at_high + high_half * at_low).astype(BF16)
    for o in range(8):
        t = lax.rem(tm + o, 8)
        send(esb.at[t], erb.at[tm], 3, e_sem.at[0], at_z(other, t))
    for o in range(1, 8):
        t = lax.rem(tm + o, 8)
        send(esf.at[t], erf.at[tm], 3, e_sem.at[1], at_z(zh, t))
    erf[tm] = esf[tm]
    landed(8, e_sem.at[0])
    landed(7, e_sem.at[1])
    for b in range(8):
        value = erf[b].astype(F32) + erb[b].astype(F32)
        for c in range(2):
            o_ref[pl.ds(2 * b + c, 8, stride=16), :] = value[8 * c : 8 * c + 8]
    for phase in range(4):
        landed(sent[phase], out_sem.at[phase])


def body(fields, profiles, phase):
    square, twist = tables()
    dma = pltpu.SemaphoreType.DMA
    hbm_spec = pl.BlockSpec(memory_space=pltpu.HBM)
    out = pl.pallas_call(
        kernel,
        out_shape=jax.ShapeDtypeStruct((128, 128), F32),
        in_specs=[hbm_spec] * 5,
        out_specs=pl.BlockSpec(memory_space=pltpu.VMEM),
        scratch_shapes=[
            pltpu.VMEM((128, 128), F32),
            pltpu.VMEM((2048, 256), BF16),
            pltpu.VMEM((8, 128), F32),
            pltpu.VMEM((3, 256, 256), BF16),
            pltpu.VMEM((16, 128), F32),
            pltpu.VMEM((2048 // TILE, TILE, 256), BF16),
            pltpu.VMEM((2048 // TILE, 256, TILE), BF16),
            pltpu.VMEM((8, 4, 4, 2, 16, 128), BF16),
            pltpu.VMEM((8, 16, 128), BF16),
            pltpu.VMEM((8, 16, 128), BF16),
            pltpu.VMEM((16, 16, 128), BF16),
            pltpu.VMEM((8, 16, 128), BF16),
            pltpu.VMEM((16, 128), F32),
            pltpu.VMEM((256, 128), F32),
            pltpu.VMEM((512, 16, 128), BF16),
            pltpu.VMEM((8, 4, 4, 2, 16, 128), F32),
            pltpu.VMEM((8, 4, 4, 2, 16, 128), BF16),
            pltpu.VMEM((len(STRAIGHT_OUT), 15, 2, 16, 128), BF16),
            pltpu.VMEM((8, 3, 4, 2, 16, 128), BF16),
            pltpu.VMEM((8, 4, 2, 16, 128), BF16),
            pltpu.VMEM((8, 3, 2, 16, 128), BF16),
            pltpu.VMEM((8, 4, 2, 16, 128), F32),
            pltpu.VMEM((8, 2, 16, 128), F32),
            pltpu.VMEM((8, 16, 128), BF16),
            pltpu.VMEM((8, 16, 128), BF16),
            pltpu.VMEM((8, 16, 128), BF16),
            pltpu.VMEM((8, 16, 128), BF16),
            dma((5,)), dma((4,)), dma((8,)), dma((1,)), dma((1,)), dma((8, 2)), dma((8, 2)), dma((2,)),
        ],
        compiler_params=pltpu.CompilerParams(
            collective_id=0, has_side_effects=True, vmem_limit_bytes=44_000_000
        ),
    )(*[pltpu.with_memory_space_constraint(v, pltpu.HBM) for v in (fields.reshape(128, 128), profiles, phase.reshape(8, 128), jnp.asarray(square), jnp.asarray(twist))])
    return out.reshape(8, 8, 2, 128)


def solution(mesh):
    return jax.shard_map(
        body,
        mesh=mesh,
        in_specs=(P("pix", None, None, "tm"), P("pix", None), P(("pix", "tm"), None)),
        out_specs=P("pix", None, None, "tm"),
        check_vma=False,
    )
```

```python
import functools
import math

import jax
import jax.numpy as jnp
import numpy as np
from jax import lax
from jax.experimental import pallas as pl
from jax.experimental.pallas import tpu as pltpu
from jax.sharding import PartitionSpec as P

MESH = pl.DeviceIdType.MESH
F32 = jnp.float32
BF16 = jnp.bfloat16

SLOTS = ((2, 1), (2, 0), (1, 1), (1, 0), (3, 1), (3, 0), (0, 1), (0, 0))
TILE = 256
STRAIGHT_IN = (0, 1)
STRAIGHT_OUT = (6, 7)
GROUPS = ((0,), (1,), (2,), (3,), (4,), (5,), (6,), (7,))
FIRST_ORDER = (0, 2, 4, 3, 1, 5, 6, 7)
EARLY, FIRST_LAG = 2, 4
FAR_FIRST = (10, 6, 9, 11, 14, 2, 5, 7, 8, 13, 15, 1, 3, 4, 12)


def tables():
    row = np.arange(256)
    order = (row // 8 % 2) * 128 + (row // 16) * 8 + row % 8
    perm = np.zeros((256, 256), np.float32)
    perm[order, row] = 1.0
    angle = 2.0 * np.pi * (np.outer(np.arange(128), np.arange(128)) % 128) / 128.0
    cos, sin = np.cos(angle), np.sin(angle)
    dft = np.block([[cos, -sin], [sin, cos]]).astype(np.float32)
    high = dft.astype(jnp.bfloat16)
    low = (dft - high.astype(np.float32)).astype(jnp.bfloat16)
    turn = 2.0 * np.pi * np.outer(np.arange(8), np.arange(128)) / 1024.0
    twist = np.concatenate([np.cos(turn), np.sin(turn)]).astype(np.float32)
    square = np.stack([perm.astype(jnp.bfloat16), high, low])
    return square, twist


def fft8(re, im, sign):
    half = math.sqrt(0.5)

    def turned(x, y, k):
        if k == 0:
            return x, y
        if k == 1:
            return (x - sign * y) * half, (y + sign * x) * half
        if k == 2:
            return (-y, x) if sign > 0 else (y, -x)
        return (-x - sign * y) * half, (-y + sign * x) * half

    def four(r, i):
        ar, ai, br, bi = r[0] + r[2], i[0] + i[2], r[0] - r[2], i[0] - i[2]
        cr, ci, dr, di = r[1] + r[3], i[1] + i[3], r[1] - r[3], i[1] - i[3]
        dr, di = turned(dr, di, 2)
        return [ar + cr, br + dr, ar - cr, br - dr], [ai + ci, bi + di, ai - ci, bi - di]

    er, ei = four(re[0::2], im[0::2])
    od, oi = four(re[1::2], im[1::2])
    out_re, out_im = [None] * 8, [None] * 8
    for k in range(4):
        tr, ti = turned(od[k], oi[k], k)
        out_re[k], out_im[k] = er[k] + tr, ei[k] + ti
        out_re[k + 4], out_im[k + 4] = er[k] - tr, ei[k] - ti
    return out_re, out_im


def split(value):
    high = value.astype(BF16)
    return high, (value - high.astype(F32)).astype(BF16)


def dot(a, b, dims=((1,), (0,))):
    return lax.dot_general(a, b, (dims, ((), ())), preferred_element_type=F32)


def kernel(
    f_hbm, p_hbm, ph_hbm, sq_hbm, tw_hbm, o_ref,
    f_v, p_v, ph_v, sq_v, tw_v, pm_v, pt_v, mbuf, s_hi, s_lo, a1, lo, cs_s, cs_r,
    tile, kf, ks, krd, kr1, k1s, kr2, kmid, kx, esf, esb, erf, erb,
    in_sem, out_sem, a1r, lor, csr, a2r, c1r, e_sem,
):
    pix, tm = lax.axis_index("pix"), lax.axis_index("tm")
    zh, y, x = pix // 16, (pix // 4) % 4, pix % 4
    yx = pix % 16
    zl, core = tm // 2, tm % 2
    other = 1 - zh
    here = zh * 8 + tm

    def at_z(h, t):
        return (h * 16 + yx, t)

    def at_x(k):
        return (zh * 16 + y * 4 + lax.rem(x + k, 4), tm)

    def at_y(k):
        return (zh * 16 + lax.rem(y + k, 4) * 4 + x, tm)

    def remote(src, dst, ss, rs, device):
        return pltpu.make_async_remote_copy(
            src_ref=src, dst_ref=dst, send_sem=ss, recv_sem=rs, device_id=device, device_id_type=MESH
        )

    def at_plane(k):
        to_y, to_x = lax.rem(y + k // 4, 4), lax.rem(x + k % 4, 4)
        return to_y, to_x, (zh * 16 + to_y * 4 + to_x, tm)

    def column(o):
        peer = lax.rem(here + o, 16)
        return peer // 8, lax.rem(peer, 8)

    sent = [0] * 4

    def send(src, dst, phase, rs, device):
        remote(src, dst, out_sem.at[phase], rs, device).start()
        sent[phase] += math.prod(src.shape) * src.dtype.itemsize // 4096

    def landed(tiles, sem):
        ref = tile.at[pl.ds(0, tiles)]
        pltpu.make_async_copy(ref, ref, sem).wait()

    barrier = pltpu.get_barrier_semaphore()
    for o in (8, 7, 9, 6, 10, 5, 11, 4, 12, 3, 13, 2, 14, 1, 15):
        h, t = column(o)
        pl.semaphore_signal(barrier, inc=1, device_id=at_z(h, t), device_id_type=MESH)
    for k in range(1, 16):
        pl.semaphore_signal(barrier, inc=1, device_id=at_plane(k)[2], device_id_type=MESH)

    loads = [
        pltpu.make_async_copy(src, dst, in_sem.at[n])
        for n, (src, dst) in enumerate(
            ((f_hbm, f_v), (ph_hbm, ph_v), (sq_hbm, sq_v), (p_hbm, p_v), (tw_hbm, tw_v))
        )
    ]
    for load in loads:
        load.start()

    loads[0].wait()
    for b in range(8):
        value = jnp.concatenate([f_v[pl.ds(2 * b + c, 8, stride=16), :] for c in range(2)], axis=0)
        high, low = split(value)
        s_hi[b] = high
        s_lo[b] = low
    a1[here] = s_hi[tm]
    lo[tm] = s_lo[tm]

    pl.semaphore_wait(barrier, 30)
    for o in (8, 7, 9, 6, 10, 5, 11, 4, 12, 3, 13, 2, 14, 1, 15):
        h, t = column(o)
        send(s_hi.at[t], a1.at[here], 0, a1r.at[tm], at_z(h, t))


    loads[1].wait()
    lane = lax.broadcasted_iota(jnp.int32, (8, 128), 1)
    sub = lax.broadcasted_iota(jnp.int32, (8, 128), 0)
    chosen = lax.rem(lane, 8) == sub
    rows = []
    for k in range(8):
        spread = jnp.where(chosen, jnp.broadcast_to(ph_v[k : k + 1, :], (8, 128)), 0.0)
        first, rest = split(spread)
        second = rest.astype(F32)
        third = spread - first.astype(F32) - second
        rows += [first.astype(F32), second, third]
    gather_lane = lax.broadcasted_iota(jnp.int32, (128, 128), 0) // 8
    gather = (gather_lane == lax.broadcasted_iota(jnp.int32, (128, 128), 1)).astype(F32).astype(BF16)
    packed = dot(jnp.concatenate(rows, axis=0).astype(BF16), gather)
    angle = jnp.zeros((8, 128), F32)
    for k in range(8):
        part = packed[24 * k : 24 * k + 8] + packed[24 * k + 8 : 24 * k + 16] + packed[24 * k + 16 : 24 * k + 24]
        angle = angle + (part if k == 0 else pltpu.roll(part, 16 * k, 1))
    cs_s[0:8, :] = jnp.cos(angle)
    cs_s[8:16, :] = jnp.sin(angle)
    mine = pl.ds(pl.multiple_of(here * 16, 16), 16)
    cs_r[mine, :] = cs_s[...]

    for n in range(2, 5):
        loads[n].wait()
    for n in range(2048 // TILE):
        block = p_v[n * TILE : (n + 1) * TILE, :]
        pm_v[n] = dot(block, sq_v[0]).astype(BF16)
        pt_v[n] = dot(sq_v[0], block, ((0,), (1,))).astype(BF16)

    blocks = [lax.rem(zl + step, 4) * 2 + c for step, c in SLOTS]

    def first_leg(n):
        a = blocks[n]
        if n < 6:
            landed(2, a1r.at[a])
        elif n == 6:
            landed(2, a1r.at[zl * 2 + 1 - core])
            landed(1, a1r.at[tm])
        first, second = a1[a].astype(F32), a1[8 + a].astype(F32)
        for c in range(2):
            both = jnp.concatenate([first[8 * c : 8 * c + 8], second[8 * c : 8 * c + 8]], axis=0)
            mbuf[a, y, x, c] = both.astype(BF16)
        piece = mbuf.at[a, y, x]
        if n in STRAIGHT_IN:
            for k in FAR_FIRST:
                send(piece, piece, 1, a2r.at[n, 1], at_plane(k)[2])
            return
        for k in range(1, 4):
            send(piece, piece, 1, a2r.at[n, 0], at_x(k) if n % 2 == 0 else at_y(k))

    def second_leg(n):
        a = blocks[n]
        landed(6, a2r.at[n, 0])
        piece = mbuf.at[a, y] if n % 2 == 0 else mbuf.at[a, :, x]
        for k in (2, 1, 3):
            send(piece, piece, 1, a2r.at[n, 1], at_y(k) if n % 2 == 0 else at_x(k))

    def spread(n, total):
        for c in range(2):
            half = total[:, 128 * c : 128 * c + 128].reshape(4, 4, 16, 128)
            kf[n, :, :, c] = half
            ks[n, :, :, c] = half.astype(BF16)
        if n in STRAIGHT_OUT:
            for k in FAR_FIRST:
                to_y, to_x, to = at_plane(k)
                send(ks.at[n, to_y, to_x], krd.at[STRAIGHT_OUT.index(n), k - 1], 2, c1r.at[n, 0], to)
            return
        for k in (2, 1, 3):
            if n % 2 == 0:
                piece, to = ks.at[n, :, lax.rem(x + k, 4)], at_x(k)
            else:
                piece, to = ks.at[n, lax.rem(y + k, 4)], at_y(k)
            send(piece, kr1.at[n, k - 1], 2, c1r.at[n, 0], to)

    def compute(slots):
        pieces = []
        for n in slots:
            landed(30 if n in STRAIGHT_IN else 24, a2r.at[n, 1])
            pieces += [mbuf[blocks[n], :, :, c].reshape(256, 128) for c in range(2)]
        fields = jnp.concatenate(pieces, axis=1)
        total = None
        for t in range(2048 // TILE):
            spatial = dot(pm_v[t], fields)
            cubes = []
            for at in range(0, 256 * len(slots), 256):
                re, im = spatial[:, at : at + 128], spatial[:, at + 128 : at + 256]
                power = re * re + im * im
                cubes += [power * re, power * im]
            part = dot(pt_v[t], jnp.concatenate(cubes, axis=1).astype(BF16))
            total = part if total is None else total + part
        for at, n in enumerate(slots):
            spread(n, total[:, 256 * at : 256 * at + 256])

    def reduce_first(n):
        landed(24, c1r.at[n, 0])
        total = kf[n, :, x] if n % 2 == 0 else kf[n, y]
        for k in range(3):
            total = total + kr1[n, k].astype(F32)
        kmid[n] = total
        k1s[n] = total.astype(BF16)
        for k in range(1, 4):
            if n % 2 == 0:
                piece, to = k1s.at[n, lax.rem(y + k, 4)], at_y(k)
            else:
                piece, to = k1s.at[n, lax.rem(x + k, 4)], at_x(k)
            send(piece, kr2.at[n, k - 1], 2, c1r.at[n, 1], to)

    def reduce_straight(n):
        landed(30, c1r.at[n, 0])
        total = kf[n, y, x]
        for k in range(15):
            total = total + krd[STRAIGHT_OUT.index(n), k].astype(F32)
        kx[blocks[n]] = total

    def reduce_second(n):
        landed(6, c1r.at[n, 1])
        total = kmid[n, y] if n % 2 == 0 else kmid[n, x]
        for k in range(3):
            total = total + kr2[n, k].astype(F32)
        kx[blocks[n]] = total

    for n in FIRST_ORDER:
        first_leg(n)
    for o in range(1, 8):
        t = lax.rem(tm + o, 8)
        send(s_lo.at[t], lo.at[tm], 0, lor.at[0], at_z(zh, t))
    for o in range(1, 16):
        h, t = column(o)
        send(cs_s, cs_r.at[mine], 0, csr.at[0], at_z(h, t))
    two_legs = [n for n in range(8) if n not in STRAIGHT_IN]
    out_legs = [n for n in range(8) if n not in STRAIGHT_OUT]
    for n in two_legs[:EARLY]:
        second_leg(n)
    for slots in GROUPS:
        compute(slots)
        if slots[0] == 0:
            for m in two_legs[EARLY:]:
                second_leg(m)
        for m in out_legs:
            if m + FIRST_LAG in slots:
                reduce_first(m)
    for m in out_legs:
        if m + FIRST_LAG > 7:
            reduce_first(m)
    for m in out_legs:
        reduce_second(m)
    for m in STRAIGHT_OUT:
        reduce_straight(m)

    landed(7, lor.at[0])
    landed(30, csr.at[0])
    scale = 1.0 / math.sqrt(65536.0)
    at_low = jnp.where(zh == 0, 1.0, 0.0).astype(F32)
    at_high = 1.0 - at_low
    step_re, step_im = [], []
    for a in range(8):
        own = a1[zh * 8 + a].astype(F32) + lo[a].astype(F32)
        own_re = jnp.concatenate([own[:8] * at_low, own[:8] * at_high], axis=0)
        own_im = jnp.concatenate([own[8:] * at_low, own[8:] * at_high], axis=0)
        step_re.append(own_re - kx[a, 1] * scale)
        step_im.append(own_im + kx[a, 0] * scale)
    fre, fim = fft8(step_re, step_im, -1)
    turned = []
    for r in range(8):
        cos, sin = tw_v[r : r + 1, :], tw_v[8 + r : 9 + r, :]
        turned.append(jnp.concatenate([fre[r] * cos + fim[r] * sin, fim[r] * cos - fre[r] * sin], axis=1))
    high, low = split(jnp.concatenate(turned, axis=0))
    freq = dot(high, sq_v[1]) + dot(low, sq_v[1]) + dot(high, sq_v[2])
    spun = []
    for r in range(8):
        cos, sin = cs_r[pl.ds(r, 16, stride=16), :], cs_r[pl.ds(8 + r, 16, stride=16), :]
        re, im = freq[16 * r : 16 * r + 16, :128], freq[16 * r : 16 * r + 16, 128:]
        spun.append(jnp.concatenate([re * cos - im * sin, re * sin + im * cos], axis=1))
    high, low = split(jnp.concatenate(spun, axis=0))
    back_dims = ((1,), (1,))
    back = dot(high, sq_v[1], back_dims) + dot(low, sq_v[1], back_dims) + dot(high, sq_v[2], back_dims)
    again_re, again_im = [], []
    for r in range(8):
        cos, sin = tw_v[r : r + 1, :] * (1.0 / 1024.0), tw_v[8 + r : 9 + r, :] * (1.0 / 1024.0)
        re, im = back[16 * r : 16 * r + 16, :128], back[16 * r : 16 * r + 16, 128:]
        again_re.append(re * cos - im * sin)
        again_im.append(im * cos + re * sin)
    out_re, out_im = fft8(again_re, again_im, 1)

    for a in range(8):
        low_half = jnp.concatenate([out_re[a][:8], out_im[a][:8]], axis=0)
        high_half = jnp.concatenate([out_re[a][8:], out_im[a][8:]], axis=0)
        esf[a] = (low_half * at_low + high_half * at_high).astype(BF16)
        esb[a] = (low_half * at_high + high_half * at_low).astype(BF16)
    for o in range(8):
        t = lax.rem(tm + o, 8)
        send(esb.at[t], erb.at[tm], 3, e_sem.at[0], at_z(other, t))
    for o in range(1, 8):
        t = lax.rem(tm + o, 8)
        send(esf.at[t], erf.at[tm], 3, e_sem.at[1], at_z(zh, t))
    erf[tm] = esf[tm]
    landed(8, e_sem.at[0])
    landed(7, e_sem.at[1])
    for b in range(8):
        value = erf[b].astype(F32) + erb[b].astype(F32)
        for c in range(2):
            o_ref[pl.ds(2 * b + c, 8, stride=16), :] = value[8 * c : 8 * c + 8]
    for phase in range(4):
        landed(sent[phase], out_sem.at[phase])


def body(fields, profiles, phase):
    square, twist = tables()
    dma = pltpu.SemaphoreType.DMA
    hbm_spec = pl.BlockSpec(memory_space=pltpu.HBM)
    out = pl.pallas_call(
        kernel,
        out_shape=jax.ShapeDtypeStruct((128, 128), F32),
        in_specs=[hbm_spec] * 5,
        out_specs=pl.BlockSpec(memory_space=pltpu.VMEM),
        scratch_shapes=[
            pltpu.VMEM((128, 128), F32),
            pltpu.VMEM((2048, 256), BF16),
            pltpu.VMEM((8, 128), F32),
            pltpu.VMEM((3, 256, 256), BF16),
            pltpu.VMEM((16, 128), F32),
            pltpu.VMEM((2048 // TILE, TILE, 256), BF16),
            pltpu.VMEM((2048 // TILE, 256, TILE), BF16),
            pltpu.VMEM((8, 4, 4, 2, 16, 128), BF16),
            pltpu.VMEM((8, 16, 128), BF16),
            pltpu.VMEM((8, 16, 128), BF16),
            pltpu.VMEM((16, 16, 128), BF16),
            pltpu.VMEM((8, 16, 128), BF16),
            pltpu.VMEM((16, 128), F32),
            pltpu.VMEM((256, 128), F32),
            pltpu.VMEM((512, 16, 128), BF16),
            pltpu.VMEM((8, 4, 4, 2, 16, 128), F32),
            pltpu.VMEM((8, 4, 4, 2, 16, 128), BF16),
            pltpu.VMEM((len(STRAIGHT_OUT), 15, 2, 16, 128), BF16),
            pltpu.VMEM((8, 3, 4, 2, 16, 128), BF16),
            pltpu.VMEM((8, 4, 2, 16, 128), BF16),
            pltpu.VMEM((8, 3, 2, 16, 128), BF16),
            pltpu.VMEM((8, 4, 2, 16, 128), F32),
            pltpu.VMEM((8, 2, 16, 128), F32),
            pltpu.VMEM((8, 16, 128), BF16),
            pltpu.VMEM((8, 16, 128), BF16),
            pltpu.VMEM((8, 16, 128), BF16),
            pltpu.VMEM((8, 16, 128), BF16),
            dma((5,)), dma((4,)), dma((8,)), dma((1,)), dma((1,)), dma((8, 2)), dma((8, 2)), dma((2,)),
        ],
        compiler_params=pltpu.CompilerParams(
            collective_id=0, has_side_effects=True, vmem_limit_bytes=44_000_000
        ),
    )(*[pltpu.with_memory_space_constraint(v, pltpu.HBM) for v in (fields.reshape(128, 128), profiles, phase.reshape(8, 128), jnp.asarray(square), jnp.asarray(twist))])
    return out.reshape(8, 8, 2, 128)


def solution(mesh):
    return jax.shard_map(
        body,
        mesh=mesh,
        in_specs=(P("pix", None, None, "tm"), P("pix", None), P(("pix", "tm"), None)),
        out_specs=P("pix", None, None, "tm"),
        check_vma=False,
    )
```

```python
import functools
import math

import jax
import jax.numpy as jnp
import numpy as np
from jax import lax
from jax.experimental import pallas as pl
from jax.experimental.pallas import tpu as pltpu
from jax.sharding import PartitionSpec as P

MESH = pl.DeviceIdType.MESH
F32 = jnp.float32
BF16 = jnp.bfloat16

SLOTS = ((2, 1), (2, 0), (1, 1), (1, 0), (3, 1), (3, 0), (0, 1), (0, 0))
TILE = 256
STRAIGHT_IN = (0, 1)
STRAIGHT_OUT = (6, 7)
GROUPS = ((0,), (1,), (2,), (3,), (4,), (5,), (6,), (7,))
FIRST_ORDER = (0, 2, 4, 3, 1, 5, 6, 7)
EARLY, FIRST_LAG = 1, 4
FAR_FIRST = (10, 6, 9, 11, 14, 2, 5, 7, 8, 13, 15, 1, 3, 4, 12)


def tables():
    row = np.arange(256)
    order = (row // 8 % 2) * 128 + (row // 16) * 8 + row % 8
    perm = np.zeros((256, 256), np.float32)
    perm[order, row] = 1.0
    angle = 2.0 * np.pi * (np.outer(np.arange(128), np.arange(128)) % 128) / 128.0
    cos, sin = np.cos(angle), np.sin(angle)
    dft = np.block([[cos, -sin], [sin, cos]]).astype(np.float32)
    high = dft.astype(jnp.bfloat16)
    low = (dft - high.astype(np.float32)).astype(jnp.bfloat16)
    turn = 2.0 * np.pi * np.outer(np.arange(8), np.arange(128)) / 1024.0
    twist = np.concatenate([np.cos(turn), np.sin(turn)]).astype(np.float32)
    square = np.stack([perm.astype(jnp.bfloat16), high, low])
    return square, twist


def fft8(re, im, sign):
    half = math.sqrt(0.5)

    def turned(x, y, k):
        if k == 0:
            return x, y
        if k == 1:
            return (x - sign * y) * half, (y + sign * x) * half
        if k == 2:
            return (-y, x) if sign > 0 else (y, -x)
        return (-x - sign * y) * half, (-y + sign * x) * half

    def four(r, i):
        ar, ai, br, bi = r[0] + r[2], i[0] + i[2], r[0] - r[2], i[0] - i[2]
        cr, ci, dr, di = r[1] + r[3], i[1] + i[3], r[1] - r[3], i[1] - i[3]
        dr, di = turned(dr, di, 2)
        return [ar + cr, br + dr, ar - cr, br - dr], [ai + ci, bi + di, ai - ci, bi - di]

    er, ei = four(re[0::2], im[0::2])
    od, oi = four(re[1::2], im[1::2])
    out_re, out_im = [None] * 8, [None] * 8
    for k in range(4):
        tr, ti = turned(od[k], oi[k], k)
        out_re[k], out_im[k] = er[k] + tr, ei[k] + ti
        out_re[k + 4], out_im[k + 4] = er[k] - tr, ei[k] - ti
    return out_re, out_im


def split(value):
    high = value.astype(BF16)
    return high, (value - high.astype(F32)).astype(BF16)


def dot(a, b, dims=((1,), (0,))):
    return lax.dot_general(a, b, (dims, ((), ())), preferred_element_type=F32)


def kernel(
    f_hbm, p_hbm, ph_hbm, sq_hbm, tw_hbm, o_ref,
    f_v, p_v, ph_v, sq_v, tw_v, pm_v, pt_v, mbuf, s_hi, s_lo, a1, lo, cs_s, cs_r,
    tile, kf, ks, krd, kr1, k1s, kr2, kmid, kx, esf, esb, erf, erb,
    in_sem, out_sem, a1r, lor, csr, a2r, c1r, e_sem,
):
    pix, tm = lax.axis_index("pix"), lax.axis_index("tm")
    zh, y, x = pix // 16, (pix // 4) % 4, pix % 4
    yx = pix % 16
    zl, core = tm // 2, tm % 2
    other = 1 - zh
    here = zh * 8 + tm

    def at_z(h, t):
        return (h * 16 + yx, t)

    def at_x(k):
        return (zh * 16 + y * 4 + lax.rem(x + k, 4), tm)

    def at_y(k):
        return (zh * 16 + lax.rem(y + k, 4) * 4 + x, tm)

    def remote(src, dst, ss, rs, device):
        return pltpu.make_async_remote_copy(
            src_ref=src, dst_ref=dst, send_sem=ss, recv_sem=rs, device_id=device, device_id_type=MESH
        )

    def at_plane(k):
        to_y, to_x = lax.rem(y + k // 4, 4), lax.rem(x + k % 4, 4)
        return to_y, to_x, (zh * 16 + to_y * 4 + to_x, tm)

    def column(o):
        peer = lax.rem(here + o, 16)
        return peer // 8, lax.rem(peer, 8)

    sent = [0] * 4

    def send(src, dst, phase, rs, device):
        remote(src, dst, out_sem.at[phase], rs, device).start()
        sent[phase] += math.prod(src.shape) * src.dtype.itemsize // 4096

    def landed(tiles, sem):
        ref = tile.at[pl.ds(0, tiles)]
        pltpu.make_async_copy(ref, ref, sem).wait()

    barrier = pltpu.get_barrier_semaphore()
    for o in (8, 7, 9, 6, 10, 5, 11, 4, 12, 3, 13, 2, 14, 1, 15):
        h, t = column(o)
        pl.semaphore_signal(barrier, inc=1, device_id=at_z(h, t), device_id_type=MESH)
    for k in range(1, 16):
        pl.semaphore_signal(barrier, inc=1, device_id=at_plane(k)[2], device_id_type=MESH)

    loads = [
        pltpu.make_async_copy(src, dst, in_sem.at[n])
        for n, (src, dst) in enumerate(
            ((f_hbm, f_v), (ph_hbm, ph_v), (sq_hbm, sq_v), (p_hbm, p_v), (tw_hbm, tw_v))
        )
    ]
    for load in loads:
        load.start()

    loads[0].wait()
    for b in range(8):
        value = jnp.concatenate([f_v[pl.ds(2 * b + c, 8, stride=16), :] for c in range(2)], axis=0)
        high, low = split(value)
        s_hi[b] = high
        s_lo[b] = low
    a1[here] = s_hi[tm]
    lo[tm] = s_lo[tm]

    pl.semaphore_wait(barrier, 30)
    for o in (8, 7, 9, 6, 10, 5, 11, 4, 12, 3, 13, 2, 14, 1, 15):
        h, t = column(o)
        send(s_hi.at[t], a1.at[here], 0, a1r.at[tm], at_z(h, t))


    loads[1].wait()
    lane = lax.broadcasted_iota(jnp.int32, (8, 128), 1)
    sub = lax.broadcasted_iota(jnp.int32, (8, 128), 0)
    chosen = lax.rem(lane, 8) == sub
    rows = []
    for k in range(8):
        spread = jnp.where(chosen, jnp.broadcast_to(ph_v[k : k + 1, :], (8, 128)), 0.0)
        first, rest = split(spread)
        second = rest.astype(F32)
        third = spread - first.astype(F32) - second
        rows += [first.astype(F32), second, third]
    gather_lane = lax.broadcasted_iota(jnp.int32, (128, 128), 0) // 8
    gather = (gather_lane == lax.broadcasted_iota(jnp.int32, (128, 128), 1)).astype(F32).astype(BF16)
    packed = dot(jnp.concatenate(rows, axis=0).astype(BF16), gather)
    angle = jnp.zeros((8, 128), F32)
    for k in range(8):
        part = packed[24 * k : 24 * k + 8] + packed[24 * k + 8 : 24 * k + 16] + packed[24 * k + 16 : 24 * k + 24]
        angle = angle + (part if k == 0 else pltpu.roll(part, 16 * k, 1))
    cs_s[0:8, :] = jnp.cos(angle)
    cs_s[8:16, :] = jnp.sin(angle)
    mine = pl.ds(pl.multiple_of(here * 16, 16), 16)
    cs_r[mine, :] = cs_s[...]

    for n in range(2, 5):
        loads[n].wait()
    for n in range(2048 // TILE):
        block = p_v[n * TILE : (n + 1) * TILE, :]
        pm_v[n] = dot(block, sq_v[0]).astype(BF16)
        pt_v[n] = dot(sq_v[0], block, ((0,), (1,))).astype(BF16)

    blocks = [lax.rem(zl + step, 4) * 2 + c for step, c in SLOTS]

    def first_leg(n):
        a = blocks[n]
        if n < 6:
            landed(2, a1r.at[a])
        elif n == 6:
            landed(2, a1r.at[zl * 2 + 1 - core])
            landed(1, a1r.at[tm])
        first, second = a1[a].astype(F32), a1[8 + a].astype(F32)
        for c in range(2):
            both = jnp.concatenate([first[8 * c : 8 * c + 8], second[8 * c : 8 * c + 8]], axis=0)
            mbuf[a, y, x, c] = both.astype(BF16)
        piece = mbuf.at[a, y, x]
        if n in STRAIGHT_IN:
            for k in FAR_FIRST:
                send(piece, piece, 1, a2r.at[n, 1], at_plane(k)[2])
            return
        for k in range(1, 4):
            send(piece, piece, 1, a2r.at[n, 0], at_x(k) if n % 2 == 0 else at_y(k))

    def second_leg(n):
        a = blocks[n]
        landed(6, a2r.at[n, 0])
        piece = mbuf.at[a, y] if n % 2 == 0 else mbuf.at[a, :, x]
        for k in (2, 1, 3):
            send(piece, piece, 1, a2r.at[n, 1], at_y(k) if n % 2 == 0 else at_x(k))

    def spread(n, total):
        for c in range(2):
            half = total[:, 128 * c : 128 * c + 128].reshape(4, 4, 16, 128)
            kf[n, :, :, c] = half
            ks[n, :, :, c] = half.astype(BF16)
        if n in STRAIGHT_OUT:
            for k in FAR_FIRST:
                to_y, to_x, to = at_plane(k)
                send(ks.at[n, to_y, to_x], krd.at[STRAIGHT_OUT.index(n), k - 1], 2, c1r.at[n, 0], to)
            return
        for k in (2, 1, 3):
            if n % 2 == 0:
                piece, to = ks.at[n, :, lax.rem(x + k, 4)], at_x(k)
            else:
                piece, to = ks.at[n, lax.rem(y + k, 4)], at_y(k)
            send(piece, kr1.at[n, k - 1], 2, c1r.at[n, 0], to)

    def compute(slots):
        pieces = []
        for n in slots:
            landed(30 if n in STRAIGHT_IN else 24, a2r.at[n, 1])
            pieces += [mbuf[blocks[n], :, :, c].reshape(256, 128) for c in range(2)]
        fields = jnp.concatenate(pieces, axis=1)
        total = None
        for t in range(2048 // TILE):
            spatial = dot(pm_v[t], fields)
            cubes = []
            for at in range(0, 256 * len(slots), 256):
                re, im = spatial[:, at : at + 128], spatial[:, at + 128 : at + 256]
                power = re * re + im * im
                cubes += [power * re, power * im]
            part = dot(pt_v[t], jnp.concatenate(cubes, axis=1).astype(BF16))
            total = part if total is None else total + part
        for at, n in enumerate(slots):
            spread(n, total[:, 256 * at : 256 * at + 256])

    def reduce_first(n):
        landed(24, c1r.at[n, 0])
        total = kf[n, :, x] if n % 2 == 0 else kf[n, y]
        for k in range(3):
            total = total + kr1[n, k].astype(F32)
        kmid[n] = total
        k1s[n] = total.astype(BF16)
        for k in range(1, 4):
            if n % 2 == 0:
                piece, to = k1s.at[n, lax.rem(y + k, 4)], at_y(k)
            else:
                piece, to = k1s.at[n, lax.rem(x + k, 4)], at_x(k)
            send(piece, kr2.at[n, k - 1], 2, c1r.at[n, 1], to)

    def reduce_straight(n):
        landed(30, c1r.at[n, 0])
        total = kf[n, y, x]
        for k in range(15):
            total = total + krd[STRAIGHT_OUT.index(n), k].astype(F32)
        kx[blocks[n]] = total

    def reduce_second(n):
        landed(6, c1r.at[n, 1])
        total = kmid[n, y] if n % 2 == 0 else kmid[n, x]
        for k in range(3):
            total = total + kr2[n, k].astype(F32)
        kx[blocks[n]] = total

    for n in FIRST_ORDER:
        first_leg(n)
    for o in range(1, 8):
        t = lax.rem(tm + o, 8)
        send(s_lo.at[t], lo.at[tm], 0, lor.at[0], at_z(zh, t))
    for o in range(1, 16):
        h, t = column(o)
        send(cs_s, cs_r.at[mine], 0, csr.at[0], at_z(h, t))
    two_legs = [n for n in range(8) if n not in STRAIGHT_IN]
    out_legs = [n for n in range(8) if n not in STRAIGHT_OUT]
    for n in two_legs[:EARLY]:
        second_leg(n)
    for slots in GROUPS:
        compute(slots)
        if slots[0] == 0:
            for m in two_legs[EARLY:]:
                second_leg(m)
        for m in out_legs:
            if m + FIRST_LAG in slots:
                reduce_first(m)
    for m in out_legs:
        if m + FIRST_LAG > 7:
            reduce_first(m)
    for m in out_legs:
        reduce_second(m)
    for m in STRAIGHT_OUT:
        reduce_straight(m)

    landed(7, lor.at[0])
    landed(30, csr.at[0])
    scale = 1.0 / math.sqrt(65536.0)
    at_low = jnp.where(zh == 0, 1.0, 0.0).astype(F32)
    at_high = 1.0 - at_low
    step_re, step_im = [], []
    for a in range(8):
        own = a1[zh * 8 + a].astype(F32) + lo[a].astype(F32)
        own_re = jnp.concatenate([own[:8] * at_low, own[:8] * at_high], axis=0)
        own_im = jnp.concatenate([own[8:] * at_low, own[8:] * at_high], axis=0)
        step_re.append(own_re - kx[a, 1] * scale)
        step_im.append(own_im + kx[a, 0] * scale)
    fre, fim = fft8(step_re, step_im, -1)
    turned = []
    for r in range(8):
        cos, sin = tw_v[r : r + 1, :], tw_v[8 + r : 9 + r, :]
        turned.append(jnp.concatenate([fre[r] * cos + fim[r] * sin, fim[r] * cos - fre[r] * sin], axis=1))
    high, low = split(jnp.concatenate(turned, axis=0))
    freq = dot(high, sq_v[1]) + dot(low, sq_v[1]) + dot(high, sq_v[2])
    spun = []
    for r in range(8):
        cos, sin = cs_r[pl.ds(r, 16, stride=16), :], cs_r[pl.ds(8 + r, 16, stride=16), :]
        re, im = freq[16 * r : 16 * r + 16, :128], freq[16 * r : 16 * r + 16, 128:]
        spun.append(jnp.concatenate([re * cos - im * sin, re * sin + im * cos], axis=1))
    high, low = split(jnp.concatenate(spun, axis=0))
    back_dims = ((1,), (1,))
    back = dot(high, sq_v[1], back_dims) + dot(low, sq_v[1], back_dims) + dot(high, sq_v[2], back_dims)
    again_re, again_im = [], []
    for r in range(8):
        cos, sin = tw_v[r : r + 1, :] * (1.0 / 1024.0), tw_v[8 + r : 9 + r, :] * (1.0 / 1024.0)
        re, im = back[16 * r : 16 * r + 16, :128], back[16 * r : 16 * r + 16, 128:]
        again_re.append(re * cos - im * sin)
        again_im.append(im * cos + re * sin)
    out_re, out_im = fft8(again_re, again_im, 1)

    for a in range(8):
        low_half = jnp.concatenate([out_re[a][:8], out_im[a][:8]], axis=0)
        high_half = jnp.concatenate([out_re[a][8:], out_im[a][8:]], axis=0)
        esf[a] = (low_half * at_low + high_half * at_high).astype(BF16)
        esb[a] = (low_half * at_high + high_half * at_low).astype(BF16)
    for o in range(8):
        t = lax.rem(tm + o, 8)
        send(esb.at[t], erb.at[tm], 3, e_sem.at[0], at_z(other, t))
    for o in range(1, 8):
        t = lax.rem(tm + o, 8)
        send(esf.at[t], erf.at[tm], 3, e_sem.at[1], at_z(zh, t))
    erf[tm] = esf[tm]
    landed(8, e_sem.at[0])
    landed(7, e_sem.at[1])
    for b in range(8):
        value = erf[b].astype(F32) + erb[b].astype(F32)
        for c in range(2):
            o_ref[pl.ds(2 * b + c, 8, stride=16), :] = value[8 * c : 8 * c + 8]
    for phase in range(4):
        landed(sent[phase], out_sem.at[phase])


def body(fields, profiles, phase):
    square, twist = tables()
    dma = pltpu.SemaphoreType.DMA
    hbm_spec = pl.BlockSpec(memory_space=pltpu.HBM)
    out = pl.pallas_call(
        kernel,
        out_shape=jax.ShapeDtypeStruct((128, 128), F32),
        in_specs=[hbm_spec] * 5,
        out_specs=pl.BlockSpec(memory_space=pltpu.VMEM),
        scratch_shapes=[
            pltpu.VMEM((128, 128), F32),
            pltpu.VMEM((2048, 256), BF16),
            pltpu.VMEM((8, 128), F32),
            pltpu.VMEM((3, 256, 256), BF16),
            pltpu.VMEM((16, 128), F32),
            pltpu.VMEM((2048 // TILE, TILE, 256), BF16),
            pltpu.VMEM((2048 // TILE, 256, TILE), BF16),
            pltpu.VMEM((8, 4, 4, 2, 16, 128), BF16),
            pltpu.VMEM((8, 16, 128), BF16),
            pltpu.VMEM((8, 16, 128), BF16),
            pltpu.VMEM((16, 16, 128), BF16),
            pltpu.VMEM((8, 16, 128), BF16),
            pltpu.VMEM((16, 128), F32),
            pltpu.VMEM((256, 128), F32),
            pltpu.VMEM((512, 16, 128), BF16),
            pltpu.VMEM((8, 4, 4, 2, 16, 128), F32),
            pltpu.VMEM((8, 4, 4, 2, 16, 128), BF16),
            pltpu.VMEM((len(STRAIGHT_OUT), 15, 2, 16, 128), BF16),
            pltpu.VMEM((8, 3, 4, 2, 16, 128), BF16),
            pltpu.VMEM((8, 4, 2, 16, 128), BF16),
            pltpu.VMEM((8, 3, 2, 16, 128), BF16),
            pltpu.VMEM((8, 4, 2, 16, 128), F32),
            pltpu.VMEM((8, 2, 16, 128), F32),
            pltpu.VMEM((8, 16, 128), BF16),
            pltpu.VMEM((8, 16, 128), BF16),
            pltpu.VMEM((8, 16, 128), BF16),
            pltpu.VMEM((8, 16, 128), BF16),
            dma((5,)), dma((4,)), dma((8,)), dma((1,)), dma((1,)), dma((8, 2)), dma((8, 2)), dma((2,)),
        ],
        compiler_params=pltpu.CompilerParams(
            collective_id=0, has_side_effects=True, vmem_limit_bytes=44_000_000
        ),
    )(*[pltpu.with_memory_space_constraint(v, pltpu.HBM) for v in (fields.reshape(128, 128), profiles, phase.reshape(8, 128), jnp.asarray(square), jnp.asarray(twist))])
    return out.reshape(8, 8, 2, 128)


def solution(mesh):
    return jax.shard_map(
        body,
        mesh=mesh,
        in_specs=(P("pix", None, None, "tm"), P("pix", None), P(("pix", "tm"), None)),
        out_specs=P("pix", None, None, "tm"),
        check_vma=False,
    )
```
